32 devices in a mesh: dp: 8 (over z, x), feat: 4 (over y, core).
Axes of the slice: x: 2, y: 2, z: 4, core: 2. Of those that a mesh axis runs over, the one named last changes fastest.
Arguments:
- member_feats: bfloat16 [32768, 256], P(('dp', 'feat')), may hold values from -6 to 6
- labels: int32 [32768], P(('dp', 'feat')), may hold values 0 or 1
- fixed_values: bfloat16 [32768, 2048], P('dp', 'feat'), may hold values from -6 to 6
- fixed_blocks: int32 [32768, 4], P('dp', 'feat'), may hold values from 0 to 511
- fixed_coef: float32 [2048, 512], P('feat'), may hold values from -0.12 to 0.12
- member_coef: float32 [128, 256], P(('dp', 'feat')), may hold values from -0.36 to 0.36
- row_slot: int32 [32768], P(('dp', 'feat')), may hold values from 0 to 2047, as said below
- tile_source: int32 [77824], P(('dp', 'feat')), may hold values from 0 to 2048, as said below
- member_tiles: int32 [128], P(('dp', 'feat')), may hold values from 1 to 16, as said below
Outputs:
- margin: float32 [32768], P(('dp', 'feat'))
- updated_coef: float32 [128, 256], P(('dp', 'feat'))
- fixed_grad: float32 [2048, 512], P('feat')
The draws below stay inside these ranges and needn't reach their ends.
Inputs may be any that keep to these rules, and one draw needn't show every extreme that they name: `row_slot`: each owner receives the same number of rows, 256, 128 or 64, from every device of its feat column; some owner receives 256 from every device. The rows one device sends to one owner take that owner's slots 0, 1, 2 and so on, each slot once. `tile_source`: every received row appears at exactly one position. An owner's members, in order, take consecutive runs of tiles; a member's rows fill its tiles from the first position on, and the rest of its last tile is padding, as are the tiles past all members. `member_tiles`: A member's tiles are its received rows divided by 128, rounded up; a device's members use at most 19 tiles in all, exactly 19 on the owners that receive 256 rows from every device.
All inputs are finite; a program needn't handle non-finite values. No bound on the sum of `labels` on one device may be relied on, other than what follows from the above.
Results may differ from the reference program's by a relative error of at most 0.0013.
Values may be sent and summed in bfloat16 or wider, within the bound.
No kernel may reach another device: no remote copies, remote signals or barrier semaphores. Data moves between devices by JAX's collectives and lax.ppermute only.
A program may use at most 64 MiB of HBM per device.

```python
import jax
import jax.numpy as jnp
from jax import lax

RE_DIM = 256
BLOCK = 512
FE_BLOCKS = 2048
ROWS_DEV = 1024
MEM_DEV = 4
CG_ITERS = 2
TILE = 128
CAP = 256
TILES_DEV = 19
ROWS = 32768
MEMBERS = 128
FE_COLS = 2048
N_DP = 8
N_FEAT = 4


def layout(key):
    device_total = N_DP * N_FEAT
    slot_total = N_DP * CAP
    tiled_rows = TILES_DEV * TILE
    level_table = jnp.array([CAP, CAP // 2, CAP // 4, CAP // 4], dtype=jnp.int32)
    column_keys = jax.random.split(jax.random.fold_in(key, 1), N_FEAT)

    def column_classes(column_key):
        shuffled = jax.random.permutation(column_key, N_DP).astype(jnp.int32)
        return ((shuffled - shuffled[N_DP - 1]) % 4).astype(jnp.int32)
    classes = jax.vmap(column_classes)(column_keys)
    counts = level_table[classes]
    sender_keys = jax.random.split(jax.random.fold_in(key, 2), device_total)
    owner_keys = jax.random.split(jax.random.fold_in(key, 3), device_total)

    def sender(sender_key, device):
        per_owner = counts[device % N_FEAT]
        owner_ends = jnp.cumsum(per_owner)
        ordinal = jnp.arange(ROWS_DEV, dtype=jnp.int32)
        owner_index = jnp.sum((ordinal[:, None] >= owner_ends[None, :]).astype(jnp.int32), axis=1)
        slot_index = ordinal - (owner_ends - per_owner)[owner_index]
        slot_value = (owner_index * CAP + slot_index).astype(jnp.int32)
        shuffle = jax.random.permutation(sender_key, ROWS_DEV)
        return jnp.zeros((ROWS_DEV,), jnp.int32).at[shuffle].set(slot_value)

    def owner_side(owner_key, device):
        per_source = counts[device % N_FEAT, device // N_FEAT]
        received = N_DP * per_source
        most_extra = jnp.maximum(0, (received - MEM_DEV) // (TILE * (MEM_DEV - 1)))
        extra_tiles = jax.random.randint(owner_key, (MEM_DEV - 1,), 0, most_extra + 1).astype(jnp.int32)
        keep_extra = (device // N_FEAT != N_DP - 1).astype(jnp.int32)
        extra_tiles = (extra_tiles * keep_extra).astype(jnp.int32)
        leading_rows = TILE * extra_tiles + 1
        member_rows = jnp.concatenate([leading_rows, (received - jnp.sum(leading_rows))[None]]).astype(jnp.int32)
        tiles_of = ((member_rows + TILE - 1) // TILE).astype(jnp.int32)
        row_ends = jnp.cumsum(member_rows)
        row_start = row_ends - member_rows
        tile_start = jnp.cumsum(tiles_of) - tiles_of
        ordinal = jnp.arange(slot_total, dtype=jnp.int32)
        is_valid = ordinal < received
        member_index = jnp.minimum(jnp.sum((ordinal[:, None] >= row_ends[None, :]).astype(jnp.int32), axis=1), MEM_DEV - 1)
        position = tile_start[member_index] * TILE + ordinal - row_start[member_index]
        position = jnp.where(is_valid, position, tiled_rows).astype(jnp.int32)
        source_slot = (ordinal // per_source * CAP + ordinal % per_source).astype(jnp.int32)
        source_table = jnp.full((tiled_rows,), slot_total, jnp.int32).at[position].set(source_slot, mode='drop')
        return (source_table, tiles_of)
    devices = jnp.arange(device_total, dtype=jnp.int32)
    row_slot = jax.vmap(sender)(sender_keys, devices).reshape(-1)
    source_table, tiles_of = jax.vmap(owner_side)(owner_keys, devices)
    return (row_slot, source_table.reshape(-1), tiles_of.reshape(-1))


def draw_row_slot(key, part):
    return layout(jax.random.fold_in(key, 17))[0]


def draw_tile_source(key, part):
    return layout(jax.random.fold_in(key, 17))[1]


def draw_member_tiles(key, part):
    return layout(jax.random.fold_in(key, 17))[2]


def touch_ends(result, stream_key, least, top_value):
    shape = result.shape
    place = [jax.random.randint(jax.random.fold_in(stream_key, axis), (), 0, shape[axis]) for axis in range(len(shape))]
    result = result.at[tuple(place)].set(least)
    longest = shape.index(max(shape))
    place[longest] = (place[longest] + 1) % shape[longest]
    return result.at[tuple(place)].set(top_value)


def block_levels(own_key, shape, pieces, least, high):
    def one(dim, shards_of):
        steps = jax.random.uniform(jax.random.fold_in(jax.random.fold_in(own_key, 6), dim), (shards_of,), jnp.float32, least / len(pieces), high / len(pieces))
        return jnp.repeat(jnp.exp(steps), shape[dim] // shards_of).reshape((-1,) + (1,) * (len(shape) - dim - 1))

    level = one(*pieces[0])
    for cut in pieces[1:]:
        level = level * one(*cut)
    return level


def normal_values(key, dims, spread, most, cuts=(), held_as=jnp.bfloat16):
    result = jax.random.normal(key, dims, jnp.float32) * spread
    if len(cuts) > 0:
        result = block_levels(key, dims, cuts, -0.22, 0.18) * result
    return jnp.clip(result, min=-most, max=most).astype(held_as)


def setup_inputs(seed: int = 0) -> dict:
    streams_of = jax.random.split(jax.random.key(seed), 10)
    return {
        "member_feats": normal_values(streams_of[0], (ROWS, RE_DIM), 1.0, 6.0, ((0, 32),)),
        "labels": touch_ends((jax.random.randint(streams_of[1], (ROWS,), 0, 4) < 1).astype(jnp.int32), jax.random.fold_in(streams_of[1], 1), 0, 1),
        "fixed_values": normal_values(streams_of[2], (ROWS, FE_COLS), 1.0, 6.0, ((0, 8), (1, 4))),
        "fixed_blocks": touch_ends(jax.random.randint(streams_of[3], (ROWS, N_FEAT), 0, FE_BLOCKS // N_FEAT), jax.random.fold_in(streams_of[3], 1), 0, (FE_BLOCKS // N_FEAT) - 1).astype(jnp.int32),
        "fixed_coef": normal_values(streams_of[4], (FE_BLOCKS, BLOCK), 0.02, 0.12, ((0, 4),), jnp.float32),
        "member_coef": normal_values(streams_of[5], (MEMBERS, RE_DIM), 0.06, 0.36, ((0, 32),), jnp.float32),
        "row_slot": draw_row_slot(jax.random.fold_in(streams_of[9], 71), 0),
        "tile_source": draw_tile_source(jax.random.fold_in(streams_of[9], 71), 0),
        "member_tiles": draw_member_tiles(jax.random.fold_in(streams_of[9], 71), 0),
    }


ridge_member = 1.0
ridge_fixed = 1.0
highest = lax.Precision.HIGHEST

def member_update(tiled_feats, tiled_fixed, tiled_label, coef, tile_counts):
    tile_total = tiled_feats.shape[0] // TILE
    feats_wide = tiled_feats.astype(jnp.float32).reshape(tile_total, TILE, RE_DIM)
    tile_fixed = tiled_fixed.astype(jnp.float32).reshape(tile_total, TILE)
    tile_label = tiled_label.astype(jnp.float32).reshape(tile_total, TILE)
    tile_ends = jnp.cumsum(tile_counts)
    positions = jnp.arange(tile_total, dtype=jnp.int32)
    member_index = lax.optimization_barrier(jnp.sum((positions[:, None] >= tile_ends[None, :]).astype(jnp.int32), axis=1))
    tile_member = (member_index[:, None] == jnp.arange(MEM_DEV, dtype=jnp.int32)[None, :]).astype(jnp.float32)
    tile_coef = jnp.dot(tile_member, coef, precision=highest)
    logits = tile_fixed + jnp.einsum('tri,ti->tr', feats_wide, tile_coef, precision=highest)
    probability = jax.nn.sigmoid(logits)
    weight = probability * (1.0 - probability)
    gradient = jnp.dot(tile_member.T, jnp.einsum('tr,tri->ti', tile_label - probability, feats_wide, precision=highest), precision=highest) - ridge_member * coef
    diagonal = jnp.dot(tile_member.T, jnp.einsum('tr,tri->ti', weight, feats_wide * feats_wide, precision=highest), precision=highest) + ridge_member
    weighted = feats_wide * weight[:, :, None]
    tile_grams = jnp.einsum('tri,trj->tij', feats_wide, weighted, precision=highest)
    hessian = jnp.einsum('tm,tij->mij', tile_member, tile_grams, precision=highest)
    step_sum = jnp.zeros_like(coef)
    remain = gradient
    scaled = remain / diagonal
    search = scaled
    inner_product = lax.optimization_barrier(jnp.sum(remain * scaled, axis=1))
    for iteration in range(CG_ITERS):
        image = jnp.einsum('mij,mj->mi', hessian, search, precision=highest) + ridge_member * search
        alpha_step = inner_product / lax.optimization_barrier(jnp.sum(search * image, axis=1))
        step_sum = step_sum + alpha_step[:, None] * search
        if iteration + 1 < CG_ITERS:
            remain = remain - alpha_step[:, None] * image
            scaled = remain / diagonal
            inner_next = lax.optimization_barrier(jnp.sum(remain * scaled, axis=1))
            search = scaled + (inner_next / inner_product)[:, None] * search
            inner_product = inner_next
    updated = coef + step_sum
    new_scores = jnp.einsum('tri,ti->tr', feats_wide, jnp.dot(tile_member, updated, precision=highest), precision=highest)
    return (updated, new_scores.reshape(-1))

def reference(member_feats, labels, fixed_values, fixed_blocks, fixed_coef, member_coef, row_slot, tile_source, member_tiles):
    shard_blocks = FE_BLOCKS // N_FEAT
    group_rows = N_FEAT * ROWS_DEV
    slot_total = N_DP * CAP
    device_total = N_DP * N_FEAT
    coef_shards = fixed_coef.reshape(N_FEAT, shard_blocks, BLOCK)

    def group_score(operands):
        values, indices = operands
        values = values.reshape(group_rows, N_FEAT, BLOCK)
        total = jnp.zeros((group_rows,), jnp.float32)
        for shard in range(N_FEAT):
            looked_up = jnp.take(coef_shards[shard], indices[:, shard], axis=0)
            total = total + lax.optimization_barrier(jnp.sum(values[:, shard, :].astype(jnp.float32) * looked_up, axis=1))
        return total
    fixed_score = lax.map(group_score, (fixed_values.reshape(N_DP, group_rows, N_FEAT * BLOCK), fixed_blocks.reshape(N_DP, group_rows, N_FEAT))).reshape(ROWS)
    row_device = (jnp.arange(ROWS, dtype=jnp.int32) // ROWS_DEV).astype(jnp.int32)
    owner_device = row_slot // CAP * N_FEAT + row_device % N_FEAT
    received_at = row_device // N_FEAT * CAP + row_slot % CAP
    flat_index = (owner_device * (slot_total + 1) + received_at).astype(jnp.int32)
    recv_feats = jnp.zeros((device_total * (slot_total + 1), RE_DIM), jnp.bfloat16).at[flat_index].set(member_feats).reshape(device_total, slot_total + 1, RE_DIM)
    recv_score = jnp.zeros((device_total * (slot_total + 1),), jnp.bfloat16).at[flat_index].set(fixed_score.astype(jnp.bfloat16)).reshape(device_total, slot_total + 1)
    recv_label = jnp.zeros((device_total * (slot_total + 1),), jnp.bfloat16).at[flat_index].set(labels.astype(jnp.bfloat16)).reshape(device_total, slot_total + 1)

    def owner_work(operands):
        feats_here, score_here, label_here, source_here, coef_here, count_here = operands
        updated, new_scores = member_update(feats_here[source_here], score_here[source_here], label_here[source_here], coef_here, count_here)
        back = jnp.zeros((slot_total + 1,), jnp.float32).at[source_here].set(new_scores)
        return (updated, back)
    updated_coef, back = lax.map(owner_work, (recv_feats, recv_score, recv_label, tile_source.reshape(device_total, TILES_DEV * TILE), member_coef.reshape(device_total, MEM_DEV, RE_DIM), member_tiles.reshape(device_total, MEM_DEV)))
    member_score = back.reshape(-1)[flat_index]
    margin = fixed_score + member_score
    residual = labels.astype(jnp.float32) - jax.nn.sigmoid(margin)

    def group_grad(carry, operands):
        values, indices, group_residual = operands
        values = values.reshape(group_rows, N_FEAT, BLOCK)
        parts = jnp.stack([jax.ops.segment_sum(group_residual[:, None] * values[:, shard, :].astype(jnp.float32), indices[:, shard], num_segments=shard_blocks) for shard in range(N_FEAT)])
        return (carry + parts, None)
    total_grad, unused = lax.scan(group_grad, jnp.zeros((N_FEAT, shard_blocks, BLOCK), jnp.float32), (fixed_values.reshape(N_DP, group_rows, N_FEAT * BLOCK), fixed_blocks.reshape(N_DP, group_rows, N_FEAT), residual.reshape(N_DP, group_rows)))
    fixed_grad = ridge_fixed * fixed_coef - total_grad.reshape(FE_BLOCKS, BLOCK) / N_DP
    return (margin, updated_coef.reshape(MEMBERS, RE_DIM), fixed_grad)
```

```python
import jax
import jax.numpy as jnp
from jax import lax
from jax.experimental import pallas as pl
from jax.experimental.pallas import tpu as pltpu
from jax.sharding import PartitionSpec as P

CG_ITERS = 2
TILE = 128

ridge_member = 1.0
ridge_fixed = 1.0
bf16 = jnp.bfloat16
f32 = jnp.float32
f16 = jnp.float16


def split(value, parts):
    out = []
    for _ in range(parts):
        piece = value.astype(bf16)
        out.append(piece)
        value = value - piece.astype(f32)
    return out


def dot_nt(a, b):
    return lax.dot_general(a, b, (((1,), (1,)), ((), ())), preferred_element_type=f32)


def dot_nn(a, b):
    return jnp.dot(a, b, preferred_element_type=f32)


def rows_iota(shape):
    return lax.broadcasted_iota(jnp.int32, shape, 0)


def hot(index, count):
    return rows_iota((count, index.shape[1])) == index


def sigmoid(x):
    return 1.0 / (1.0 + jnp.exp(-x))


def partial_kernel(values_ref, block_ref, coef_ref, out_ref, high_ref, low_ref):
    @pl.when(pl.program_id(0) == 0)
    def _():
        high, low = split(coef_ref[...], 2)
        high_ref[...] = high
        low_ref[...] = low

    values = values_ref[...]
    product = dot_nt(high_ref[...], values) + dot_nt(low_ref[...], values)
    mask = hot(block_ref[...], product.shape[0])
    out_ref[...] = jnp.sum(jnp.where(mask, product, 0.0), axis=0, keepdims=True)


def partial_scores(fixed_values, block_row, fixed_coef):
    rows, width = fixed_values.shape
    blocks = fixed_coef.shape[0]
    step = min(512, rows)
    return pl.pallas_call(
        partial_kernel,
        grid=(rows // step,),
        in_specs=[
            pl.BlockSpec((step, width), lambda i: (i, 0)),
            pl.BlockSpec((1, step), lambda i: (0, i)),
            pl.BlockSpec((blocks, width), lambda i: (0, 0)),
        ],
        out_specs=pl.BlockSpec((1, step), lambda i: (0, i)),
        out_shape=jax.ShapeDtypeStruct((1, rows), f32),
        scratch_shapes=[pltpu.VMEM((blocks, width), bf16)] * 2,
        cost_estimate=pl.CostEstimate(
            flops=4 * rows * blocks * width,
            bytes_accessed=2 * rows * width + 4 * blocks * width,
            transcendentals=0,
        ),
        name="partial_scores",
    )(fixed_values, block_row, fixed_coef)


def grad_kernel(values_ref, block_ref, residual_ref, out_ref):
    high, low = split(residual_ref[...], 2)
    mask = hot(block_ref[...], out_ref.shape[0])
    zero = jnp.zeros((), f32)
    left_high = jnp.where(mask, high.astype(f32), zero).astype(bf16)
    left_low = jnp.where(mask, low.astype(f32), zero).astype(bf16)
    values = values_ref[...]
    total = dot_nn(left_high, values) + dot_nn(left_low, values)

    @pl.when(pl.program_id(0) == 0)
    def _():
        out_ref[...] = total

    @pl.when(pl.program_id(0) > 0)
    def _():
        out_ref[...] += total


def gradient_partial(fixed_values, block_row, residual_row, blocks):
    rows, width = fixed_values.shape
    step = min(512, rows)
    return pl.pallas_call(
        grad_kernel,
        grid=(rows // step,),
        in_specs=[
            pl.BlockSpec((step, width), lambda i: (i, 0)),
            pl.BlockSpec((1, step), lambda i: (0, i)),
            pl.BlockSpec((1, step), lambda i: (0, i)),
        ],
        out_specs=pl.BlockSpec((blocks, width), lambda i: (0, 0)),
        out_shape=jax.ShapeDtypeStruct((blocks, width), f32),
        cost_estimate=pl.CostEstimate(
            flops=4 * rows * blocks * width,
            bytes_accessed=2 * rows * width + 4 * blocks * width,
            transcendentals=0,
        ),
        name="gradient_partial",
    )(fixed_values, block_row, residual_row)


def pack_kernel(feats_ref, slot_ref, out_ref):
    count = out_ref.shape[0]
    start = pl.program_id(0) * count
    mask = (rows_iota((count, slot_ref.shape[1])) + start) == slot_ref[...]
    one_hot = jnp.where(mask, 1.0, 0.0).astype(bf16)
    out_ref[...] = dot_nn(one_hot, feats_ref[...]).astype(bf16)


def pack_feats(member_feats, slot_row, slot_total):
    rows, width = member_feats.shape
    step = min(512, slot_total)
    return pl.pallas_call(
        pack_kernel,
        grid=(slot_total // step,),
        in_specs=[
            pl.BlockSpec((rows, width), lambda i: (0, 0)),
            pl.BlockSpec((1, rows), lambda i: (0, 0)),
        ],
        out_specs=pl.BlockSpec((step, width), lambda i: (i, 0)),
        out_shape=jax.ShapeDtypeStruct((slot_total, width), bf16),
        cost_estimate=pl.CostEstimate(
            flops=2 * rows * slot_total * width,
            bytes_accessed=2 * rows * width + 2 * slot_total * width,
            transcendentals=0,
        ),
        name="pack_feats",
    )(member_feats, slot_row)


def message_kernel(capacity, parts_refs, label_ref, slot_ref, fixed_ref, out_ref):
    fixed = parts_refs[0][...]
    for part in parts_refs[1:]:
        fixed = fixed + part[...]
    fixed_ref[...] = fixed
    destinations = out_ref.shape[1]
    slot = slot_ref[...]
    owner = slot // capacity
    owner_hot = hot(owner, destinations)
    place_hot = jnp.where(hot(slot - owner * capacity, capacity), 1.0, 0.0).astype(bf16)
    score = fixed.astype(bf16).astype(f32)
    label = label_ref[...].astype(f32)
    out_ref[0] = dot_nt(jnp.where(owner_hot, score, 0.0).astype(bf16), place_hot).astype(bf16)
    out_ref[1] = dot_nt(jnp.where(owner_hot, label, 0.0).astype(bf16), place_hot).astype(bf16)


def build_message(parts, label_row, slot_row, dp_count, capacity):
    rows = slot_row.shape[1]

    def kernel(*refs):
        message_kernel(capacity, refs[: len(parts)], *refs[len(parts) :])

    return pl.pallas_call(
        kernel,
        out_shape=(
            jax.ShapeDtypeStruct((1, rows), f32),
            jax.ShapeDtypeStruct((2, dp_count, capacity), bf16),
        ),
        name="build_message",
    )(*parts, label_row, slot_row)


def slot_member_kernel(tiles_ref, source_ref, out_ref):
    slots, capacity = out_ref.shape
    source = source_ref[...]
    position = lax.broadcasted_iota(jnp.int32, source.shape, 1) // TILE
    member = jnp.zeros(source.shape, jnp.int32)
    end = jnp.int32(0)
    for m in range(tiles_ref.shape[0]):
        end = end + tiles_ref[m]
        member = member + (position >= end).astype(jnp.int32)
    sender = source // capacity
    sender_hot = jnp.where(hot(sender, slots), member.astype(f32) + 1.0, 0.0).astype(bf16)
    place_hot = jnp.where(hot(source - sender * capacity, capacity), 1.0, 0.0).astype(bf16)
    out_ref[...] = dot_nt(sender_hot, place_hot) - 1.0


def slot_members(member_tiles, source_row, dp_count, capacity):
    return pl.pallas_call(
        slot_member_kernel,
        in_specs=[
            pl.BlockSpec(memory_space=pltpu.SMEM),
            pl.BlockSpec(memory_space=pltpu.VMEM),
        ],
        out_specs=pl.BlockSpec(memory_space=pltpu.VMEM),
        out_shape=jax.ShapeDtypeStruct((dp_count, capacity), f32),
        name="slot_members",
    )(member_tiles, source_row)


def solve_kernel(feats_ref, score_ref, label_ref, member_ref, coef_ref, updated_ref, scores_ref):
    feats = feats_ref[...]
    coef = coef_ref[...]
    count = coef.shape[0]
    slots = feats.shape[0]
    own = rows_iota((count, slots)).astype(f32) == member_ref[...]

    def pick(vectors):
        high, low = split(vectors, 2)
        both = dot_nt(jnp.concatenate([high, low], axis=0), feats)
        each = both[:count] + both[count:]
        return jnp.sum(jnp.where(own, each, 0.0), axis=0, keepdims=True)

    def spread(row_weights):
        high, low = split(jnp.where(own, row_weights, 0.0), 2)
        return jnp.concatenate([high, low], axis=0)

    def gather(row_weights):
        both = dot_nn(spread(row_weights), feats)
        return both[:count] + both[count:]

    base = pick(coef)
    logits = score_ref[...].astype(f32) + base
    probability = sigmoid(logits)
    weight = probability * (1.0 - probability)
    gradient = gather(label_ref[...].astype(f32) - probability) - ridge_member * coef
    wide = feats.astype(f32)
    square_high, square_low = split(wide * wide, 2)
    weights = spread(weight)
    both = dot_nn(weights, square_high) + dot_nn(weights, square_low)
    diagonal = both[:count] + both[count:] + ridge_member
    step_sum = jnp.zeros_like(coef)
    new_scores = base
    remain = gradient
    scaled = remain / diagonal
    search = scaled
    inner_product = jnp.sum(remain * scaled, axis=1, keepdims=True)
    for iteration in range(CG_ITERS):
        projected = pick(search)
        if iteration + 1 < CG_ITERS:
            image = gather(weight * projected) + ridge_member * search
            curvature = jnp.sum(search * image, axis=1, keepdims=True)
        else:
            row_part = jnp.where(own, weight * projected * projected, 0.0)
            curvature = jnp.sum(row_part, axis=1, keepdims=True) + ridge_member * jnp.sum(
                search * search, axis=1, keepdims=True
            )
        alpha_step = inner_product / curvature
        step_sum = step_sum + alpha_step * search
        row_alpha = jnp.sum(jnp.where(own, alpha_step, 0.0), axis=0, keepdims=True)
        new_scores = new_scores + row_alpha * projected
        if iteration + 1 < CG_ITERS:
            remain = remain - alpha_step * image
            scaled = remain / diagonal
            inner_next = jnp.sum(remain * scaled, axis=1, keepdims=True)
            search = scaled + (inner_next / inner_product) * search
            inner_product = inner_next
    updated_ref[...] = coef + step_sum
    scores_ref[...] = new_scores


def solve_members(feats, score_row, label_row, member_row, member_coef):
    slots, width = feats.shape
    return pl.pallas_call(
        solve_kernel,
        out_shape=(
            jax.ShapeDtypeStruct(member_coef.shape, f32),
            jax.ShapeDtypeStruct((1, slots), f32),
        ),
        name="solve_members",
    )(feats, score_row, label_row, member_row, member_coef)


def margin_kernel(returned_ref, slot_ref, fixed_ref, label_ref, margin_ref, residual_ref):
    owners, capacity = returned_ref.shape
    slot = slot_ref[...]
    owner = slot // capacity
    place_hot = jnp.where(hot(slot - owner * capacity, capacity), 1.0, 0.0).astype(bf16)
    looked_up = jnp.zeros((owners, slot.shape[1]), f32)
    for piece in reversed(split(returned_ref[...], 3)):
        looked_up = looked_up + dot_nn(piece, place_hot)
    score = jnp.sum(jnp.where(hot(owner, owners), looked_up, 0.0), axis=0, keepdims=True)
    margin = fixed_ref[...] + score
    margin_ref[...] = margin
    residual_ref[...] = label_ref[...].astype(f32) - sigmoid(margin)


def margins(returned, slot_row, fixed_row, label_row):
    out = jax.ShapeDtypeStruct(slot_row.shape, f32)
    return pl.pallas_call(margin_kernel, out_shape=(out, out), name="margins")(
        returned, slot_row, fixed_row, label_row
    )


def swap(value, axis, offset, count):
    return lax.ppermute(value, axis, [(i, i ^ offset) for i in range(count)])


def pick_index(value, index, axis=0):
    return lax.dynamic_index_in_dim(value, index, axis, keepdims=False)


def reduce_chunks(partial, dp_count):
    half = dp_count // 2
    if half > 4 or dp_count % 2:
        sent = lax.all_to_all(partial.astype(f16), "dp", 0, 0, tiled=True)
        return jnp.sum(sent.astype(f32), axis=0)
    me = lax.axis_index("dp")
    side = me % 2
    place = me // 2
    pairs = partial.reshape((half, 2) + partial.shape[1:])
    other = swap(pick_index(pairs, 1 - side, 1).astype(f16), "dp", 1, dp_count)
    kept = pick_index(pairs, side, 1) + other.astype(f32)
    sends = kept.astype(f16)
    total = pick_index(kept, place)
    for k in range(1, half):
        got = swap(pick_index(sends, place ^ k), "dp", 2 * k, dp_count)
        total = total + got.astype(f32)
    return total


def spread_chunks(chunk, dp_count, coef, scale):
    rows, width = chunk.shape
    half = dp_count // 2
    if half > 4 or dp_count % 2:
        whole = lax.all_gather(chunk, "dp", axis=0, tiled=True)
        return ridge_fixed * coef - whole.astype(f32) * scale
    me = lax.axis_index("dp")
    side = me % 2
    place = me // 2
    other = swap(chunk, "dp", 1, dp_count)
    pair = jnp.where(
        side == 0, jnp.concatenate([chunk, other]), jnp.concatenate([other, chunk])
    )
    out = jnp.zeros(coef.shape, f32)
    for k in range(half):
        got = pair if k == 0 else swap(pair, "dp", 2 * k, dp_count)
        at = (place ^ k) * 2 * rows
        own_coef = lax.dynamic_slice_in_dim(coef, at, 2 * rows, 0)
        out = lax.dynamic_update_slice_in_dim(
            out, ridge_fixed * own_coef - got.astype(f32) * scale, at, 0
        )
    return out


def body(
    member_feats,
    labels,
    fixed_values,
    fixed_blocks,
    fixed_coef,
    member_coef,
    row_slot,
    tile_source,
    member_tiles,
):
    dp_count = lax.axis_size("dp")
    feat_count = lax.axis_size("feat")
    feat = lax.axis_index("feat")
    rows_here = member_feats.shape[0]
    blocks, block_width = fixed_coef.shape
    capacity = 2 * rows_here // dp_count
    slot_total = dp_count * capacity
    group_rows = fixed_values.shape[0]

    slot_row = row_slot.reshape(1, rows_here)
    label_row = labels.reshape(1, rows_here)
    block_row = fixed_blocks.reshape(1, group_rows)

    send_feats = pack_feats(member_feats, slot_row, slot_total)
    got_feats = lax.all_to_all(
        send_feats.reshape(dp_count, capacity, -1), "dp", split_axis=0, concat_axis=0, tiled=True
    ).reshape(slot_total, -1)
    member_row = slot_members(
        member_tiles, tile_source.reshape(1, -1), dp_count, capacity
    ).reshape(1, slot_total)

    partial = partial_scores(fixed_values, block_row, fixed_coef)

    def rows_of(shard):
        return lax.dynamic_slice_in_dim(partial, shard * rows_here, rows_here, 1)

    parts = [rows_of(feat)] + [
        swap(rows_of(feat ^ k), "feat", k, feat_count) for k in range(1, feat_count)
    ]
    fixed_row, message = build_message(parts, label_row, slot_row, dp_count, capacity)
    got = lax.all_to_all(message, "dp", split_axis=1, concat_axis=1, tiled=True)
    score_row = got[0].reshape(1, slot_total)
    tile_label = got[1].reshape(1, slot_total)

    updated_coef, new_scores = solve_members(
        got_feats, score_row, tile_label, member_row, member_coef
    )
    returned = lax.all_to_all(
        new_scores.reshape(dp_count, capacity), "dp", split_axis=0, concat_axis=0, tiled=True
    )
    margin, residual = margins(returned, slot_row, fixed_row, label_row)

    group = jnp.zeros((feat_count, rows_here), f32)
    for k in range(feat_count):
        got_residual = residual if k == 0 else swap(residual, "feat", k, feat_count)
        group = lax.dynamic_update_slice_in_dim(group, got_residual, feat ^ k, 0)
    contribution = gradient_partial(
        fixed_values, block_row, group.reshape(1, group_rows), blocks
    )
    summed = reduce_chunks(
        contribution.reshape(dp_count, blocks // dp_count, block_width) * (1.0 / dp_count), dp_count
    )
    fixed_grad = spread_chunks(summed.astype(f16), dp_count, fixed_coef, 1.0)
    return (margin.reshape(rows_here), updated_coef, fixed_grad)


def solution(mesh):
    placed = (
        P(("dp", "feat"), None),
        P(("dp", "feat")),
        P("dp", "feat"),
        P("dp", "feat"),
        P("feat", None),
        P(("dp", "feat"), None),
        P(("dp", "feat")),
        P(("dp", "feat")),
        P(("dp", "feat")),
    )
    return jax.shard_map(
        body,
        mesh=mesh,
        in_specs=placed,
        out_specs=(P(("dp", "feat")), P(("dp", "feat"), None), P("feat", None)),
        check_vma=False,
    )
```

```python
import jax
import jax.numpy as jnp
from jax import lax
from jax.experimental import pallas as pl
from jax.experimental.pallas import tpu as pltpu
from jax.sharding import PartitionSpec as P

CG_ITERS = 2
TILE = 128

ridge_member = 1.0
ridge_fixed = 1.0
bf16 = jnp.bfloat16
f32 = jnp.float32
f16 = jnp.float16


def split(value, parts):
    out = []
    for _ in range(parts):
        piece = value.astype(bf16)
        out.append(piece)
        value = value - piece.astype(f32)
    return out


def dot_nt(a, b):
    return lax.dot_general(a, b, (((1,), (1,)), ((), ())), preferred_element_type=f32)


def dot_nn(a, b):
    return jnp.dot(a, b, preferred_element_type=f32)


def rows_iota(shape):
    return lax.broadcasted_iota(jnp.int32, shape, 0)


def hot(index, count):
    return rows_iota((count, index.shape[1])) == index


def sigmoid(x):
    return 1.0 / (1.0 + jnp.exp(-x))


def partial_kernel(values_ref, block_ref, coef_ref, *refs):
    outs, (high_ref, low_ref) = refs[:-2], refs[-2:]

    @pl.when(pl.program_id(0) == 0)
    def _():
        high, low = split(coef_ref[...], 2)
        high_ref[...] = high
        low_ref[...] = low

    values = values_ref[...]
    product = dot_nt(high_ref[...], values) + dot_nt(low_ref[...], values)
    mask = hot(block_ref[...], product.shape[0])
    score = jnp.sum(jnp.where(mask, product, 0.0), axis=0, keepdims=True)
    target = pl.program_id(0) ^ lax.axis_index("feat")
    for k, out_ref in enumerate(outs):

        @pl.when(target == k)
        def _():
            out_ref[...] = score


def partial_scores(fixed_values, block_row, fixed_coef, rows_here):
    rows, width = fixed_values.shape
    blocks = fixed_coef.shape[0]
    shards = rows // rows_here
    return pl.pallas_call(
        partial_kernel,
        grid=(shards,),
        in_specs=[
            pl.BlockSpec((rows_here, width), lambda i: (i, 0)),
            pl.BlockSpec((1, rows_here), lambda i: (0, i)),
            pl.BlockSpec((blocks, width), lambda i: (0, 0)),
        ],
        out_specs=[pl.BlockSpec((1, rows_here), lambda i: (0, 0))] * shards,
        out_shape=[jax.ShapeDtypeStruct((1, rows_here), f32)] * shards,
        scratch_shapes=[pltpu.VMEM((blocks, width), bf16)] * 2,
        cost_estimate=pl.CostEstimate(
            flops=4 * rows * blocks * width,
            bytes_accessed=2 * rows * width + 4 * blocks * width,
            transcendentals=0,
        ),
        name="partial_scores",
    )(fixed_values, block_row, fixed_coef)


def grad_kernel(flip, dp_count, values_ref, block_ref, *refs):
    pieces, out_ref = refs[:-1], refs[-1]
    kept = out_ref.shape[0]
    chunk = 2 * kept // dp_count
    rows = pieces[0].shape[1]
    parity = (lax.axis_index("dp") + flip) % 2
    feat = lax.axis_index("feat")
    for k, piece in enumerate(pieces):
        at = pl.ds(pl.multiple_of((feat ^ k) * rows, rows), rows)
        block = block_ref[:, at]
        local = (block // (2 * chunk)) * chunk + block % chunk
        local = jnp.where((block // chunk) % 2 == parity, local, -1)
        mask = hot(local, kept)
        high, low = split(piece[...], 2)
        left_high = jnp.where(mask, high.astype(f32), 0.0).astype(bf16)
        left_low = jnp.where(mask, low.astype(f32), 0.0).astype(bf16)
        values = values_ref[at, :]
        total = dot_nn(left_high, values) + dot_nn(left_low, values)
        if k == 0:
            out_ref[...] = total
        else:
            out_ref[...] += total


def gradient_partial(flip, dp_count, fixed_values, block_row, pieces, blocks):
    rows, width = fixed_values.shape

    def kernel(*refs):
        grad_kernel(flip, dp_count, *refs)

    return pl.pallas_call(
        kernel,
        out_shape=jax.ShapeDtypeStruct((blocks // 2, width), f32),
        cost_estimate=pl.CostEstimate(
            flops=2 * rows * blocks * width,
            bytes_accessed=2 * rows * width + 2 * blocks * width,
            transcendentals=0,
        ),
        compiler_params=pltpu.CompilerParams(vmem_limit_bytes=24 << 20),
    )(fixed_values, block_row, *pieces)


def pack_kernel(feats_ref, slot_ref, out_ref):
    count = out_ref.shape[0]
    start = pl.program_id(0) * count
    mask = (rows_iota((count, slot_ref.shape[1])) + start) == slot_ref[...]
    one_hot = jnp.where(mask, 1.0, 0.0).astype(bf16)
    out_ref[...] = dot_nn(one_hot, feats_ref[...]).astype(bf16)


def pack_feats(member_feats, slot_row, slot_total):
    rows, width = member_feats.shape
    step = min(1024, slot_total)
    return pl.pallas_call(
        pack_kernel,
        grid=(slot_total // step,),
        in_specs=[
            pl.BlockSpec((rows, width), lambda i: (0, 0)),
            pl.BlockSpec((1, rows), lambda i: (0, 0)),
        ],
        out_specs=pl.BlockSpec((step, width), lambda i: (i, 0)),
        out_shape=jax.ShapeDtypeStruct((slot_total, width), bf16),
        cost_estimate=pl.CostEstimate(
            flops=2 * rows * slot_total * width,
            bytes_accessed=2 * rows * width + 2 * slot_total * width,
            transcendentals=0,
        ),
        name="pack_feats",
    )(member_feats, slot_row)


def message_kernel(parts_refs, label_ref, slot_ref, fixed_ref, out_ref):
    fixed = parts_refs[0][...]
    for part in parts_refs[1:]:
        fixed = fixed + part[...]
    fixed_ref[...] = fixed
    destinations, _, capacity = out_ref.shape
    slot = slot_ref[...]
    owner = slot // capacity
    owner_hot = hot(owner, destinations)
    place_hot = jnp.where(hot(slot - owner * capacity, capacity), 1.0, 0.0).astype(bf16)
    score = fixed.astype(bf16).astype(f32)
    label = label_ref[...].astype(f32)
    both = jnp.concatenate(
        [jnp.where(owner_hot, score, 0.0), jnp.where(owner_hot, label, 0.0)], axis=0
    )
    placed = dot_nt(both.astype(bf16), place_hot)
    out_ref[:, 0, :] = placed[:destinations]
    out_ref[:, 1, :] = placed[destinations:]


def build_message(parts, label_row, slot_row, dp_count, capacity):
    rows = slot_row.shape[1]

    def kernel(*refs):
        message_kernel(refs[: len(parts)], *refs[len(parts) :])

    return pl.pallas_call(
        kernel,
        out_shape=(
            jax.ShapeDtypeStruct((1, rows), f32),
            jax.ShapeDtypeStruct((dp_count, 2, capacity), f32),
        ),
        name="build_message",
    )(*parts, label_row, slot_row)


def slot_member_kernel(tiles_ref, source_ref, out_ref):
    slots, capacity = out_ref.shape
    source = source_ref[...]
    position = lax.broadcasted_iota(jnp.int32, source.shape, 1) // TILE
    member = jnp.zeros(source.shape, jnp.int32)
    end = jnp.int32(0)
    for m in range(tiles_ref.shape[0]):
        end = end + tiles_ref[m]
        member = member + (position >= end).astype(jnp.int32)
    sender = source // capacity
    sender_hot = jnp.where(hot(sender, slots), member.astype(f32) + 1.0, 0.0).astype(bf16)
    place_hot = jnp.where(hot(source - sender * capacity, capacity), 1.0, 0.0).astype(bf16)
    out_ref[...] = dot_nt(sender_hot, place_hot) - 1.0


def slot_members(member_tiles, source_row, dp_count, capacity):
    return pl.pallas_call(
        slot_member_kernel,
        in_specs=[
            pl.BlockSpec(memory_space=pltpu.SMEM),
            pl.BlockSpec(memory_space=pltpu.VMEM),
        ],
        out_specs=pl.BlockSpec(memory_space=pltpu.VMEM),
        out_shape=jax.ShapeDtypeStruct((dp_count, capacity), f32),
        name="slot_members",
    )(member_tiles, source_row)


def lane_row(pieces):
    lanes = pieces.shape[-1]
    pieces = pieces.reshape(-1, lanes)
    return jnp.concatenate([pieces[i : i + 1] for i in range(pieces.shape[0])], axis=1)


def solve_kernel(feats_ref, message_ref, member_ref, coef_ref, updated_ref, scores_ref):
    feats = feats_ref[...]
    coef = coef_ref[...]
    count = coef.shape[0]
    slots = feats.shape[0]
    lanes = message_ref.shape[2]
    message = message_ref[...]
    sent_score = lane_row(message[:, 0, :])
    label = lane_row(message[:, 1, :])
    own = rows_iota((count, slots)).astype(f32) == lane_row(member_ref[...])

    def pick(vectors):
        high, low = split(vectors, 2)
        both = dot_nt(jnp.concatenate([high, low], axis=0), feats)
        each = both[:count] + both[count:]
        return jnp.sum(jnp.where(own, each, 0.0), axis=0, keepdims=True)

    def spread(row_weights):
        high, low = split(jnp.where(own, row_weights, 0.0), 2)
        return jnp.concatenate([high, low], axis=0)

    def gather(row_weights):
        both = dot_nn(spread(row_weights), feats)
        return both[:count] + both[count:]

    base = pick(coef)
    logits = sent_score + base
    probability = sigmoid(logits)
    weight = probability * (1.0 - probability)
    gradient = gather(label - probability) - ridge_member * coef
    wide = feats.astype(f32)
    square_high, square_low = split(wide * wide, 2)
    weights = spread(weight)
    both = dot_nn(weights, square_high) + dot_nn(weights, square_low)
    diagonal = both[:count] + both[count:] + ridge_member
    step_sum = jnp.zeros_like(coef)
    new_scores = base
    remain = gradient
    scaled = remain / diagonal
    search = scaled
    inner_product = jnp.sum(remain * scaled, axis=1, keepdims=True)
    for iteration in range(CG_ITERS):
        projected = pick(search)
        if iteration + 1 < CG_ITERS:
            image = gather(weight * projected) + ridge_member * search
            curvature = jnp.sum(search * image, axis=1, keepdims=True)
        else:
            row_part = jnp.where(own, weight * projected * projected, 0.0)
            curvature = jnp.sum(row_part, axis=1, keepdims=True) + ridge_member * jnp.sum(
                search * search, axis=1, keepdims=True
            )
        alpha_step = inner_product / curvature
        step_sum = step_sum + alpha_step * search
        row_alpha = jnp.sum(jnp.where(own, alpha_step, 0.0), axis=0, keepdims=True)
        new_scores = new_scores + row_alpha * projected
        if iteration + 1 < CG_ITERS:
            remain = remain - alpha_step * image
            scaled = remain / diagonal
            inner_next = jnp.sum(remain * scaled, axis=1, keepdims=True)
            search = scaled + (inner_next / inner_product) * search
            inner_product = inner_next
    updated_ref[...] = coef + step_sum
    for i in range(scores_ref.shape[0]):
        scores_ref[i] = new_scores[:, i * lanes : (i + 1) * lanes]


def solve_members(feats, message, member_slots, member_coef):
    senders, _, capacity = message.shape
    return pl.pallas_call(
        solve_kernel,
        out_shape=(
            jax.ShapeDtypeStruct(member_coef.shape, f32),
            jax.ShapeDtypeStruct((senders, 1, capacity), f32),
        ),
        name="solve_members",
    )(feats, message, member_slots, member_coef)


def margin_kernel(returned_ref, slot_ref, fixed_ref, label_ref, margin_ref, residual_ref):
    owners, _, capacity = returned_ref.shape
    slot = slot_ref[...]
    owner = slot // capacity
    place_hot = jnp.where(hot(slot - owner * capacity, capacity), 1.0, 0.0).astype(bf16)
    pieces = split(returned_ref[...].reshape(owners, capacity), 3)
    looked_up = dot_nn(jnp.concatenate(pieces, axis=0), place_hot)
    looked_up = looked_up[:owners] + (looked_up[owners : 2 * owners] + looked_up[2 * owners :])
    score = jnp.sum(jnp.where(hot(owner, owners), looked_up, 0.0), axis=0, keepdims=True)
    margin = fixed_ref[...] + score
    margin_ref[...] = margin
    residual_ref[...] = label_ref[...].astype(f32) - sigmoid(margin)


def margins(returned, slot_row, fixed_row, label_row):
    out = jax.ShapeDtypeStruct(slot_row.shape, f32)
    return pl.pallas_call(margin_kernel, out_shape=(out, out), name="margins")(
        returned, slot_row, fixed_row, label_row
    )


def swap(value, axis, offset):
    return lax.ppermute(
        value, axis, [(i, i ^ offset) for i in range(lax.axis_size(axis))]
    )


def pick_index(value, index):
    return lax.dynamic_index_in_dim(value, index, 0, keepdims=False)


def exchange(message, side, place, half):
    if half > 4:
        return lax.all_to_all(message, "dp", 0, 0, tiled=True)
    pairs = message.reshape((half, 2) + message.shape[1:])
    own = lax.dynamic_index_in_dim(pairs, side, 1, keepdims=False)
    other = swap(lax.dynamic_index_in_dim(pairs, 1 - side, 1, keepdims=False), "dp", 1)
    both = jnp.where(
        side == 0, jnp.stack([own, other], axis=1), jnp.stack([other, own], axis=1)
    )
    out = jnp.zeros_like(both)
    for k in range(half):
        entry = pick_index(both, place ^ k)
        got = entry if k == 0 else swap(entry, "dp", 2 * k)
        out = lax.dynamic_update_index_in_dim(out, got, place ^ k, 0)
    return out.reshape(message.shape)


def reduce_rest(kept, place, stride):
    count = kept.shape[0]
    if count <= 4:
        sends = kept.astype(f16)
        total = pick_index(kept, place)
        for k in range(1, count):
            got = swap(pick_index(sends, place ^ k), "dp", stride * k)
            total = total + got.astype(f32)
        return total
    low = count // 2
    top = place // low
    view = kept.reshape((2, low) + kept.shape[1:])
    got = swap(pick_index(view, 1 - top).astype(f16), "dp", stride * low)
    return reduce_rest(pick_index(view, top) + got.astype(f32), place % low, stride)


def spread_rest(pair, place, count, stride, coef):
    rows = pair.shape[0]
    out = jnp.zeros(coef.shape, f32)

    def put(out, got, at):
        own_coef = lax.dynamic_slice_in_dim(coef, at, got.shape[0], 0)
        grad = ridge_fixed * own_coef - got.astype(f32)
        return lax.dynamic_update_slice_in_dim(out, grad, at, 0)

    if count <= 4:
        for k in range(count):
            got = pair if k == 0 else swap(pair, "dp", stride * k)
            out = put(out, got, (place ^ k) * rows)
        return out
    bit = 1
    while bit < count:
        other = swap(pair, "dp", stride * bit)
        pair = jnp.where(
            (place // bit) % 2 == 0,
            jnp.concatenate([pair, other]),
            jnp.concatenate([other, pair]),
        )
        bit *= 2
    return put(out, pair, 0)


def body(
    member_feats,
    labels,
    fixed_values,
    fixed_blocks,
    fixed_coef,
    member_coef,
    row_slot,
    tile_source,
    member_tiles,
):
    dp_count = lax.axis_size("dp")
    feat_count = lax.axis_size("feat")
    rows_here = member_feats.shape[0]
    blocks, block_width = fixed_coef.shape
    capacity = 2 * rows_here // dp_count
    slot_total = dp_count * capacity
    group_rows = fixed_values.shape[0]
    side = lax.axis_index("dp") % 2
    place = lax.axis_index("dp") // 2
    half = dp_count // 2
    chunk = blocks // dp_count

    slot_row = row_slot.reshape(1, rows_here)
    label_row = labels.reshape(1, rows_here)
    block_row = fixed_blocks.reshape(1, group_rows)

    send_feats = pack_feats(member_feats, slot_row, slot_total)
    got_feats = lax.all_to_all(
        send_feats.reshape(dp_count, capacity, -1), "dp", 0, 0, tiled=True
    ).reshape(slot_total, -1)
    member_slots = slot_members(
        member_tiles, tile_source.reshape(1, -1), dp_count, capacity
    )

    sends = partial_scores(fixed_values, block_row, fixed_coef, rows_here)
    parts = [sends[0]] + [swap(sends[k], "feat", k) for k in range(1, feat_count)]
    fixed_row, message = build_message(parts, label_row, slot_row, dp_count, capacity)
    got = exchange(message, side, place, half)

    if capacity % 128:
        got = jnp.moveaxis(got, 1, 0).reshape(1, 2, slot_total)
        member_slots = member_slots.reshape(1, slot_total)
    updated_coef, new_scores = solve_members(got_feats, got, member_slots, member_coef)
    returned = lax.all_to_all(
        new_scores.reshape(dp_count, 1, capacity), "dp", 0, 0, tiled=True
    )
    margin, residual = margins(returned, slot_row, fixed_row, label_row)

    scaled = residual * (1.0 / dp_count)
    pieces = [scaled] + [swap(scaled, "feat", k) for k in range(1, feat_count)]
    theirs = gradient_partial(1, dp_count, fixed_values, block_row, pieces, blocks)
    got_half = swap(theirs.astype(f16), "dp", 1)
    mine = gradient_partial(0, dp_count, fixed_values, block_row, pieces, blocks)
    kept = mine + got_half.astype(f32)
    summed = reduce_rest(kept.reshape(half, chunk, block_width), place, 2).astype(f16)
    other = swap(summed, "dp", 1)
    pair = jnp.where(
        side == 0, jnp.concatenate([summed, other]), jnp.concatenate([other, summed])
    )
    fixed_grad = spread_rest(pair, place, half, 2, fixed_coef)
    return (margin.reshape(rows_here), updated_coef, fixed_grad)


def solution(mesh):
    placed = (
        P(("dp", "feat"), None),
        P(("dp", "feat")),
        P("dp", "feat"),
        P("dp", "feat"),
        P("feat", None),
        P(("dp", "feat"), None),
        P(("dp", "feat")),
        P(("dp", "feat")),
        P(("dp", "feat")),
    )
    return jax.shard_map(
        body,
        mesh=mesh,
        in_specs=placed,
        out_specs=(P(("dp", "feat")), P(("dp", "feat"), None), P("feat", None)),
        check_vma=False,
    )
```

```python
import jax
import jax.numpy as jnp
from jax import lax
from jax.experimental import pallas as pl
from jax.experimental.pallas import tpu as pltpu
from jax.sharding import PartitionSpec as P

CG_ITERS = 2
TILE = 128

ridge_member = 1.0
ridge_fixed = 1.0
bf16 = jnp.bfloat16
f32 = jnp.float32
f16 = jnp.float16


def split(value, parts):
    out = []
    for _ in range(parts):
        piece = value.astype(bf16)
        out.append(piece)
        value = value - piece.astype(f32)
    return out


def dot_nt(a, b):
    return lax.dot_general(a, b, (((1,), (1,)), ((), ())), preferred_element_type=f32)


def dot_nn(a, b):
    return jnp.dot(a, b, preferred_element_type=f32)


def rows_iota(shape):
    return lax.broadcasted_iota(jnp.int32, shape, 0)


def hot(index, count):
    return rows_iota((count, index.shape[1])) == index


def sigmoid(x):
    return 1.0 / (1.0 + jnp.exp(-x))


def compiler_params(mebibytes=50):
    return pltpu.CompilerParams(vmem_limit_bytes=mebibytes << 20)


def partial_kernel(
    start_ref, values_ref, block_ref, coef_ref, label_ref, slot_ref, out_ref, rest_ref, sem
):
    rows = out_ref.shape[1]
    blocks = coef_ref.shape[0]
    shards = values_ref.shape[0] // rows
    copies = [
        pltpu.make_async_copy(
            values_ref.at[pl.ds((i + 1) * rows, rows)], rest_ref.at[i], sem.at[i]
        )
        for i in range(shards - 1)
    ]
    for copy in copies:
        copy.start()
    high, low = split(coef_ref[...].T, 2)
    lanes = lax.broadcasted_iota(jnp.int32, (1, TILE), 1)
    out_ref[shards : shards + 1, :] = label_ref[...].astype(f32)
    out_ref[shards + 1 : shards + 2, :] = slot_ref[...].astype(f32)
    for i in range(shards):
        block = block_ref[:, i * rows : (i + 1) * rows]
        column = jnp.broadcast_to(block, (TILE, rows)).T
        if i > 0:
            copies[i - 1].wait()
        values = start_ref[...] if i == 0 else rest_ref[i - 1]
        product = dot_nn(values, high) + dot_nn(values, low)
        total = jnp.zeros((rows, TILE), f32)
        for at in range(0, blocks, TILE):
            total = total + jnp.where(column == lanes + at, product[:, at : at + TILE], 0.0)
        out_ref[i : i + 1, :] = jnp.sum(total.T, axis=0, keepdims=True)


def partial_scores(start, fixed_values, block_row, fixed_coef, label_row, slot_row):
    rows, width = fixed_values.shape
    rows_here = slot_row.shape[1]
    blocks = fixed_coef.shape[0]
    shards = rows // rows_here
    vmem = pl.BlockSpec(memory_space=pltpu.VMEM)
    return pl.pallas_call(
        partial_kernel,
        in_specs=[vmem, pl.BlockSpec(memory_space=pltpu.HBM)] + [vmem] * 4,
        out_specs=vmem,
        out_shape=jax.ShapeDtypeStruct((shards + 2, rows_here), f32),
        scratch_shapes=[
            pltpu.VMEM((shards - 1, rows_here, width), bf16),
            pltpu.SemaphoreType.DMA((shards - 1,)),
        ],
        cost_estimate=pl.CostEstimate(
            flops=4 * rows * blocks * width,
            bytes_accessed=2 * rows * width + 4 * blocks * width,
            transcendentals=0,
        ),
        compiler_params=compiler_params(50),
        name="partial_scores",
    )(start, fixed_values, block_row, fixed_coef, label_row, slot_row)


def add_blocks(
    flip, dp_count, values_ref, block_ref, residual_rows, out_ref, first=True
):
    kept = out_ref.shape[0]
    chunk = 2 * kept // dp_count
    rows = residual_rows[0].shape[1]
    parity = (lax.axis_index("dp") + flip) % 2
    for i, residual in enumerate(residual_rows):
        block = block_ref[:, i * rows : (i + 1) * rows]
        local = (block // (2 * chunk)) * chunk + block % chunk
        local = jnp.where((block // chunk) % 2 == parity, local, -1)
        mask = hot(local, kept)
        high, low = split(residual, 2)
        left_high = jnp.where(mask, high.astype(f32), 0.0).astype(bf16)
        left_low = jnp.where(mask, low.astype(f32), 0.0).astype(bf16)
        values = values_ref[i * rows : (i + 1) * rows, :]
        total = dot_nn(left_high, values) + dot_nn(left_low, values)
        if first is True and i == 0:
            out_ref[...] = total
        elif first is True:
            out_ref[...] += total
        else:
            out_ref[...] = jnp.where(first, 0.0, out_ref[...]) + total


def margin_kernel(
    dp_count, returned_ref, fixed_ref, label_ref, slot_ref, values_ref, block_ref,
    margin_ref, residual_ref, out_ref, all_ref, held_ref, copy_sem,
):
    copy = pltpu.make_async_copy(values_ref, held_ref, copy_sem)
    copy.start()
    sources, _, capacity = returned_ref.shape
    shards, _ = fixed_ref.shape
    pieces = split(returned_ref[...].reshape(sources, capacity), 3)
    table = jnp.concatenate(pieces, axis=0)
    residual_rows = []
    for i in range(shards):
        slot = slot_ref[i : i + 1, :].astype(jnp.int32)
        owner = slot // capacity
        place_hot = jnp.where(hot(slot - owner * capacity, capacity), 1.0, 0.0).astype(bf16)
        found = dot_nn(table, place_hot)
        found = found[:sources] + (found[sources : 2 * sources] + found[2 * sources :])
        owner_hot = hot(owner * shards + i, sources)
        score = jnp.sum(jnp.where(owner_hot, found, 0.0), axis=0, keepdims=True)
        margin = fixed_ref[i : i + 1, :] + score
        all_ref[i : i + 1, :] = margin
        residual = (label_ref[i : i + 1, :] - sigmoid(margin)) * (1.0 / dp_count)
        residual_ref[i : i + 1, :] = residual
        residual_rows.append(residual)
    margin_ref[...] = all_ref[pl.ds(lax.axis_index("feat"), 1), :]
    copy.wait()
    add_blocks(1, dp_count, held_ref, block_ref, residual_rows, out_ref)


def margins_and_theirs(returned, fixed, label, slot, fixed_values, block_row, blocks, dp_count):
    shards, rows = fixed.shape
    width = fixed_values.shape[1]

    def kernel(*refs):
        margin_kernel(dp_count, *refs)

    vmem = pl.BlockSpec(memory_space=pltpu.VMEM)
    return pl.pallas_call(
        kernel,
        in_specs=[vmem] * 4 + [pl.BlockSpec(memory_space=pltpu.HBM), vmem],
        out_specs=[vmem] * 3,
        out_shape=(
            jax.ShapeDtypeStruct((1, rows), f32),
            jax.ShapeDtypeStruct((shards, rows), f32),
            jax.ShapeDtypeStruct((blocks // 2, width), f32),
        ),
        scratch_shapes=[
            pltpu.VMEM((shards, rows), f32),
            pltpu.VMEM(fixed_values.shape, fixed_values.dtype),
            pltpu.SemaphoreType.DMA,
        ],
        compiler_params=compiler_params(50),
        name="margins_and_theirs",
    )(returned, fixed, label, slot, fixed_values, block_row)


def mine_kernel(dp_count, residual_ref, values_ref, block_ref, out_ref):
    residual = residual_ref[pl.ds(pl.program_id(0), 1), :]
    add_blocks(0, dp_count, values_ref, block_ref, [residual], out_ref, pl.program_id(0) == 0)


def gradient_mine(residual, fixed_values, block_row, blocks, dp_count):
    rows, width = fixed_values.shape
    shards, rows_here = residual.shape

    def kernel(*refs):
        mine_kernel(dp_count, *refs)

    return pl.pallas_call(
        kernel,
        grid=(shards,),
        in_specs=[
            pl.BlockSpec((shards, rows_here), lambda i: (0, 0)),
            pl.BlockSpec((rows_here, width), lambda i: (i, 0)),
            pl.BlockSpec((1, rows_here), lambda i: (0, i)),
        ],
        out_specs=pl.BlockSpec((blocks // 2, width), lambda i: (0, 0)),
        out_shape=jax.ShapeDtypeStruct((blocks // 2, width), f32),
        cost_estimate=pl.CostEstimate(
            flops=2 * rows * blocks * width,
            bytes_accessed=2 * rows * width + 2 * blocks * width,
            transcendentals=0,
        ),
        compiler_params=compiler_params(50),
        name="gradient_mine",
    )(residual, fixed_values, block_row)


def pack_kernel(values_ref, feats_ref, slot_ref, out_ref, start_ref, copy_sem):
    first = values_ref.at[pl.ds(0, start_ref.shape[0])]
    copy = pltpu.make_async_copy(first, start_ref, copy_sem)
    copy.start()
    total = out_ref.shape[0]
    step = min(1024, total)
    for start in range(0, total, step):
        mask = (rows_iota((step, slot_ref.shape[1])) + start) == slot_ref[...]
        one_hot = jnp.where(mask, 1.0, 0.0).astype(bf16)
        out_ref[start : start + step, :] = dot_nn(one_hot, feats_ref[...]).astype(bf16)
    copy.wait()


def pack_feats(fixed_values, member_feats, slot_row, slot_total):
    rows, width = member_feats.shape
    vmem = pl.BlockSpec(memory_space=pltpu.VMEM)
    return pl.pallas_call(
        pack_kernel,
        in_specs=[pl.BlockSpec(memory_space=pltpu.HBM), vmem, vmem],
        out_specs=[vmem, vmem],
        out_shape=(
            jax.ShapeDtypeStruct((slot_total, width), bf16),
            jax.ShapeDtypeStruct((rows, fixed_values.shape[1]), bf16),
        ),
        scratch_shapes=[pltpu.SemaphoreType.DMA],
        cost_estimate=pl.CostEstimate(
            flops=2 * rows * slot_total * width,
            bytes_accessed=2 * rows * width + 2 * slot_total * width,
            transcendentals=0,
        ),
        compiler_params=compiler_params(50),
        name="pack_feats",
    )(fixed_values, member_feats, slot_row)


def message_kernel(pieces, label_ref, slot_ref, fixed_ref, labels_ref, slots_ref, out_ref):
    shards = fixed_ref.shape[0]
    feat = lax.axis_index("feat")
    fixed = pieces[0][:shards, :]
    for piece in pieces[1:]:
        fixed = fixed + piece[:shards, :]
    fixed_ref[...] = fixed
    for k, piece in enumerate(pieces):
        labels_ref[pl.ds(feat ^ k, 1), :] = piece[shards : shards + 1, :]
        slots_ref[pl.ds(feat ^ k, 1), :] = piece[shards + 1 : shards + 2, :]
    destinations, _, capacity = out_ref.shape
    slot = slot_ref[...]
    owner = slot // capacity
    owner_hot = hot(owner, destinations)
    place_hot = jnp.where(hot(slot - owner * capacity, capacity), 1.0, 0.0).astype(bf16)
    score = fixed_ref[pl.ds(feat, 1), :].astype(bf16).astype(f32)
    label = label_ref[...].astype(f32)
    both = jnp.concatenate(
        [jnp.where(owner_hot, score, 0.0), jnp.where(owner_hot, label, 0.0)], axis=0
    )
    placed = dot_nt(both.astype(bf16), place_hot)
    out_ref[:, 0, :] = placed[:destinations]
    out_ref[:, 1, :] = placed[destinations:]


def build_message(pieces, label_row, slot_row, dp_count, capacity):
    rows = slot_row.shape[1]
    shards = len(pieces)

    def kernel(*refs):
        message_kernel(refs[:shards], *refs[shards:])

    return pl.pallas_call(
        kernel,
        out_shape=[jax.ShapeDtypeStruct((shards, rows), f32)] * 3
        + [jax.ShapeDtypeStruct((dp_count, 2, capacity), f32)],
        compiler_params=compiler_params(),
        name="build_message",
    )(*pieces, label_row, slot_row)


def slot_member_kernel(tiles_ref, source_ref, out_ref):
    slots, capacity = out_ref.shape
    source = source_ref[...]
    position = lax.broadcasted_iota(jnp.int32, source.shape, 1) // TILE
    member = jnp.zeros(source.shape, jnp.int32)
    end = jnp.int32(0)
    for m in range(tiles_ref.shape[0]):
        end = end + tiles_ref[m]
        member = member + (position >= end).astype(jnp.int32)
    sender = source // capacity
    sender_hot = jnp.where(hot(sender, slots), member.astype(f32) + 1.0, 0.0).astype(bf16)
    place_hot = jnp.where(hot(source - sender * capacity, capacity), 1.0, 0.0).astype(bf16)
    out_ref[...] = dot_nt(sender_hot, place_hot) - 1.0


def slot_members(member_tiles, source_row, dp_count, capacity):
    return pl.pallas_call(
        slot_member_kernel,
        in_specs=[
            pl.BlockSpec(memory_space=pltpu.SMEM),
            pl.BlockSpec(memory_space=pltpu.VMEM),
        ],
        out_specs=pl.BlockSpec(memory_space=pltpu.VMEM),
        out_shape=jax.ShapeDtypeStruct((dp_count, capacity), f32),
        compiler_params=compiler_params(),
        name="slot_members",
    )(member_tiles, source_row)


def lane_row(pieces):
    lanes = pieces.shape[-1]
    pieces = pieces.reshape(-1, lanes)
    return jnp.concatenate([pieces[i : i + 1] for i in range(pieces.shape[0])], axis=1)


def solve_kernel(feats_ref, message_ref, member_ref, coef_ref, updated_ref, scores_ref):
    feats = feats_ref[...]
    coef = coef_ref[...]
    count = coef.shape[0]
    slots = feats.shape[0]
    lanes = message_ref.shape[2]
    message = message_ref[...]
    sent_score = lane_row(message[:, 0, :])
    label = lane_row(message[:, 1, :])
    own = rows_iota((count, slots)).astype(f32) == lane_row(member_ref[...])

    def pick(vectors):
        high, low = split(vectors, 2)
        both = dot_nt(jnp.concatenate([high, low], axis=0), feats)
        each = both[:count] + both[count:]
        return jnp.sum(jnp.where(own, each, 0.0), axis=0, keepdims=True)

    def spread(row_weights):
        high, low = split(jnp.where(own, row_weights, 0.0), 2)
        return jnp.concatenate([high, low], axis=0)

    def gather(row_weights):
        both = dot_nn(spread(row_weights), feats)
        return both[:count] + both[count:]

    base = pick(coef)
    logits = sent_score + base
    probability = sigmoid(logits)
    weight = probability * (1.0 - probability)
    gradient = gather(label - probability) - ridge_member * coef
    wide = feats.astype(f32)
    square_high, square_low = split(wide * wide, 2)
    weights = spread(weight)
    both = dot_nn(weights, square_high) + dot_nn(weights, square_low)
    diagonal = both[:count] + both[count:] + ridge_member
    step_sum = jnp.zeros_like(coef)
    new_scores = base
    remain = gradient
    scaled = remain / diagonal
    search = scaled
    inner_product = jnp.sum(remain * scaled, axis=1, keepdims=True)
    for iteration in range(CG_ITERS):
        projected = pick(search)
        if iteration + 1 < CG_ITERS:
            image = gather(weight * projected) + ridge_member * search
            curvature = jnp.sum(search * image, axis=1, keepdims=True)
        else:
            row_part = jnp.where(own, weight * projected * projected, 0.0)
            curvature = jnp.sum(row_part, axis=1, keepdims=True) + ridge_member * jnp.sum(
                search * search, axis=1, keepdims=True
            )
        alpha_step = inner_product / curvature
        step_sum = step_sum + alpha_step * search
        row_alpha = jnp.sum(jnp.where(own, alpha_step, 0.0), axis=0, keepdims=True)
        new_scores = new_scores + row_alpha * projected
        if iteration + 1 < CG_ITERS:
            remain = remain - alpha_step * image
            scaled = remain / diagonal
            inner_next = jnp.sum(remain * scaled, axis=1, keepdims=True)
            search = scaled + (inner_next / inner_product) * search
            inner_product = inner_next
    updated_ref[...] = coef + step_sum
    copies = scores_ref.shape[0] * lanes // slots
    for i in range(slots // lanes):
        for copy in range(copies):
            scores_ref[i * copies + copy] = new_scores[:, i * lanes : (i + 1) * lanes]


def solve_members(feats, message, member_slots, member_coef, copies):
    senders, _, capacity = message.shape
    return pl.pallas_call(
        solve_kernel,
        out_shape=(
            jax.ShapeDtypeStruct(member_coef.shape, f32),
            jax.ShapeDtypeStruct((senders * copies, 1, capacity), f32),
        ),
        compiler_params=compiler_params(),
        name="solve_members",
    )(feats, message, member_slots, member_coef)


def swap(value, axis, offset):
    return lax.ppermute(
        value, axis, [(i, i ^ offset) for i in range(lax.axis_size(axis))]
    )


def pick_index(value, index):
    return lax.dynamic_index_in_dim(value, index, 0, keepdims=False)


def exchange(message, side, place, half):
    if half > 4:
        return lax.all_to_all(message, "dp", 0, 0, tiled=True)
    pairs = message.reshape((half, 2) + message.shape[1:])
    own = lax.dynamic_index_in_dim(pairs, side, 1, keepdims=False)
    other = swap(lax.dynamic_index_in_dim(pairs, 1 - side, 1, keepdims=False), "dp", 1)
    both = jnp.where(
        side == 0, jnp.stack([own, other], axis=1), jnp.stack([other, own], axis=1)
    )
    out = jnp.zeros_like(both)
    for k in range(half):
        entry = pick_index(both, place ^ k)
        got = entry if k == 0 else swap(entry, "dp", 2 * k)
        out = lax.dynamic_update_index_in_dim(out, got, place ^ k, 0)
    return out.reshape(message.shape)


def reduce_rest(kept, place, stride):
    count = kept.shape[0]
    if count <= 4:
        sends = kept.astype(f16)
        total = pick_index(kept, place)
        for k in range(1, count):
            got = swap(pick_index(sends, place ^ k), "dp", stride * k)
            total = total + got.astype(f32)
        return total
    low = count // 2
    top = place // low
    view = kept.reshape((2, low) + kept.shape[1:])
    got = swap(pick_index(view, 1 - top).astype(f16), "dp", stride * low)
    return reduce_rest(pick_index(view, top) + got.astype(f32), place % low, stride)


def spread_rest(pair, place, count, stride, coef):
    rows = pair.shape[0]
    out = jnp.zeros(coef.shape, f32)

    def put(out, got, at):
        own_coef = lax.dynamic_slice_in_dim(coef, at, got.shape[0], 0)
        grad = ridge_fixed * own_coef - got.astype(f32)
        return lax.dynamic_update_slice_in_dim(out, grad, at, 0)

    if count <= 4:
        for k in range(count):
            got = pair if k == 0 else swap(pair, "dp", stride * k)
            out = put(out, got, (place ^ k) * rows)
        return out
    bit = 1
    while bit < count:
        other = swap(pair, "dp", stride * bit)
        pair = jnp.where(
            (place // bit) % 2 == 0,
            jnp.concatenate([pair, other]),
            jnp.concatenate([other, pair]),
        )
        bit *= 2
    return put(out, pair, 0)


def body(
    member_feats,
    labels,
    fixed_values,
    fixed_blocks,
    fixed_coef,
    member_coef,
    row_slot,
    tile_source,
    member_tiles,
):
    dp_count = lax.axis_size("dp")
    feat_count = lax.axis_size("feat")
    rows_here = member_feats.shape[0]
    blocks, block_width = fixed_coef.shape
    capacity = 2 * rows_here // dp_count
    slot_total = dp_count * capacity
    group_rows = fixed_values.shape[0]
    side = lax.axis_index("dp") % 2
    place = lax.axis_index("dp") // 2
    half = dp_count // 2
    chunk = blocks // dp_count

    slot_row = row_slot.reshape(1, rows_here)
    label_row = labels.reshape(1, rows_here)
    block_row = fixed_blocks.reshape(1, group_rows)

    send_feats, start = pack_feats(fixed_values, member_feats, slot_row, slot_total)
    got_feats = lax.all_to_all(
        send_feats.reshape(dp_count, capacity, -1), "dp", 0, 0, tiled=True
    ).reshape(slot_total, -1)
    member_slots = slot_members(
        member_tiles, tile_source.reshape(1, -1), dp_count, capacity
    )

    own = partial_scores(
        start, fixed_values, block_row, fixed_coef, label_row, slot_row
    )
    pieces = [own] + [swap(own, "feat", k) for k in range(1, feat_count)]
    fixed, label, slot, message = build_message(
        pieces, label_row, slot_row, dp_count, capacity
    )
    got = exchange(message, side, place, half)

    if capacity % 128:
        got = jnp.moveaxis(got, 1, 0).reshape(1, 2, slot_total)
        member_slots = member_slots.reshape(1, slot_total)
        updated_coef, new_scores = solve_members(got_feats, got, member_slots, member_coef, 1)
        new_scores = jnp.broadcast_to(
            new_scores.reshape(dp_count, 1, 1, capacity), (dp_count, feat_count, 1, capacity)
        ).reshape(dp_count * feat_count, 1, capacity)
    else:
        updated_coef, new_scores = solve_members(
            got_feats, got, member_slots, member_coef, feat_count
        )
    returned = lax.all_to_all(new_scores, ("dp", "feat"), 0, 0, tiled=True)
    margin, residual, theirs = margins_and_theirs(
        returned, fixed, label, slot, fixed_values, block_row, blocks, dp_count
    )
    got_half = swap(theirs.astype(f16), "dp", 1)
    mine = gradient_mine(residual, fixed_values, block_row, blocks, dp_count)
    kept = mine + got_half.astype(f32)
    summed = reduce_rest(kept.reshape(half, chunk, block_width), place, 2).astype(f16)
    other = swap(summed, "dp", 1)
    pair = jnp.where(
        side == 0, jnp.concatenate([summed, other]), jnp.concatenate([other, summed])
    )
    fixed_grad = spread_rest(pair, place, half, 2, fixed_coef)
    return (margin.reshape(rows_here), updated_coef, fixed_grad)


def solution(mesh):
    placed = (
        P(("dp", "feat"), None),
        P(("dp", "feat")),
        P("dp", "feat"),
        P("dp", "feat"),
        P("feat", None),
        P(("dp", "feat"), None),
        P(("dp", "feat")),
        P(("dp", "feat")),
        P(("dp", "feat")),
    )
    return jax.shard_map(
        body,
        mesh=mesh,
        in_specs=placed,
        out_specs=(P(("dp", "feat")), P(("dp", "feat"), None), P("feat", None)),
        check_vma=False,
    )
```

```python
import jax
import jax.numpy as jnp
from jax import lax
from jax.experimental import pallas as pl
from jax.experimental.pallas import tpu as pltpu
from jax.sharding import PartitionSpec as P

CG_ITERS = 2
TILE = 128

ridge_member = 1.0
ridge_fixed = 1.0
bf16 = jnp.bfloat16
f32 = jnp.float32
f16 = jnp.float16


def split(value, parts):
    out = []
    for _ in range(parts):
        piece = value.astype(bf16)
        out.append(piece)
        value = value - piece.astype(f32)
    return out


def dot_nt(a, b):
    return lax.dot_general(a, b, (((1,), (1,)), ((), ())), preferred_element_type=f32)


def dot_nn(a, b):
    return jnp.dot(a, b, preferred_element_type=f32)


def rows_iota(shape):
    return lax.broadcasted_iota(jnp.int32, shape, 0)


def hot(index, count):
    return rows_iota((count, index.shape[1])) == index


def sigmoid(x):
    return 1.0 / (1.0 + jnp.exp(-x))


def compiler_params(mebibytes=50):
    return pltpu.CompilerParams(vmem_limit_bytes=mebibytes << 20)


def partial_kernel(
    start_ref, values_ref, block_ref, coef_ref, label_ref, slot_ref, out_ref, rest_ref, sem
):
    rows = out_ref.shape[1]
    blocks = coef_ref.shape[0]
    shards = values_ref.shape[0] // rows
    copies = [
        pltpu.make_async_copy(
            values_ref.at[pl.ds((i + 1) * rows, rows)], rest_ref.at[i], sem.at[i]
        )
        for i in range(shards - 1)
    ]
    for copy in copies:
        copy.start()
    high, low = split(coef_ref[...].T, 2)
    lanes = lax.broadcasted_iota(jnp.int32, (1, TILE), 1)
    out_ref[shards : shards + 1, :] = label_ref[...].astype(f32)
    out_ref[shards + 1 : shards + 2, :] = slot_ref[...].astype(f32)
    for i in range(shards):
        block = block_ref[:, i * rows : (i + 1) * rows]
        column = jnp.broadcast_to(block, (TILE, rows)).T
        if i > 0:
            copies[i - 1].wait()
        values = start_ref[...] if i == 0 else rest_ref[i - 1]
        product = dot_nn(values, high) + dot_nn(values, low)
        total = jnp.zeros((rows, TILE), f32)
        for at in range(0, blocks, TILE):
            total = total + jnp.where(column == lanes + at, product[:, at : at + TILE], 0.0)
        out_ref[i : i + 1, :] = jnp.sum(total.T, axis=0, keepdims=True)


def partial_scores(start, fixed_values, block_row, fixed_coef, label_row, slot_row):
    rows, width = fixed_values.shape
    rows_here = slot_row.shape[1]
    blocks = fixed_coef.shape[0]
    shards = rows // rows_here
    vmem = pl.BlockSpec(memory_space=pltpu.VMEM)
    return pl.pallas_call(
        partial_kernel,
        in_specs=[vmem, pl.BlockSpec(memory_space=pltpu.HBM)] + [vmem] * 4,
        out_specs=vmem,
        out_shape=jax.ShapeDtypeStruct((shards + 2, rows_here), f32),
        scratch_shapes=[
            pltpu.VMEM((shards - 1, rows_here, width), bf16),
            pltpu.SemaphoreType.DMA((shards - 1,)),
        ],
        cost_estimate=pl.CostEstimate(
            flops=4 * rows * blocks * width,
            bytes_accessed=2 * rows * width + 4 * blocks * width,
            transcendentals=0,
        ),
        compiler_params=compiler_params(50),
        name="partial_scores",
    )(start, fixed_values, block_row, fixed_coef, label_row, slot_row)


def add_blocks(
    flip, dp_count, values_ref, block_ref, residual_rows, out_ref
):
    kept = out_ref.shape[0]
    chunk = 2 * kept // dp_count
    rows = residual_rows[0].shape[1]
    parity = (lax.axis_index("dp") + flip) % 2
    place = lax.axis_index("dp") // 2
    for i, residual in enumerate(residual_rows):
        block = block_ref[:, i * rows : (i + 1) * rows]
        local = ((block // (2 * chunk)) ^ place) * chunk + block % chunk
        local = jnp.where((block // chunk) % 2 == parity, local, -1)
        mask = hot(local, kept)
        high, low = split(residual, 2)
        left_high = jnp.where(mask, high.astype(f32), 0.0).astype(bf16)
        left_low = jnp.where(mask, low.astype(f32), 0.0).astype(bf16)
        values = values_ref[i * rows : (i + 1) * rows, :]
        total = dot_nn(left_high, values) + dot_nn(left_low, values)
        if i == 0:
            out_ref[...] = total
        else:
            out_ref[...] += total


def margin_kernel(
    dp_count, returned_ref, fixed_ref, label_ref, slot_ref, values_ref, block_ref,
    margin_ref, residual_ref, out_ref, held_ref, all_ref, copy_sem,
):
    copy = pltpu.make_async_copy(values_ref, held_ref, copy_sem)
    copy.start()
    sources, _, capacity = returned_ref.shape
    shards, _ = fixed_ref.shape
    pieces = split(returned_ref[...].reshape(sources, capacity), 3)
    table = jnp.concatenate(pieces, axis=0)
    residual_rows = []
    for i in range(shards):
        slot = slot_ref[i : i + 1, :].astype(jnp.int32)
        owner = slot // capacity
        place_hot = jnp.where(hot(slot - owner * capacity, capacity), 1.0, 0.0).astype(bf16)
        found = dot_nn(table, place_hot)
        found = found[:sources] + (found[sources : 2 * sources] + found[2 * sources :])
        owner_hot = hot(owner * shards + i, sources)
        score = jnp.sum(jnp.where(owner_hot, found, 0.0), axis=0, keepdims=True)
        margin = fixed_ref[i : i + 1, :] + score
        all_ref[i : i + 1, :] = margin
        residual = (label_ref[i : i + 1, :] - sigmoid(margin)) * (1.0 / dp_count)
        residual_ref[i : i + 1, :] = residual
        residual_rows.append(residual)
    margin_ref[...] = all_ref[pl.ds(lax.axis_index("feat"), 1), :]
    copy.wait()
    add_blocks(1, dp_count, held_ref, block_ref, residual_rows, out_ref)


def margins_and_theirs(returned, fixed, label, slot, fixed_values, block_row, blocks, dp_count):
    shards, rows = fixed.shape
    width = fixed_values.shape[1]

    def kernel(*refs):
        margin_kernel(dp_count, *refs)

    vmem = pl.BlockSpec(memory_space=pltpu.VMEM)
    return pl.pallas_call(
        kernel,
        in_specs=[vmem] * 4 + [pl.BlockSpec(memory_space=pltpu.HBM), vmem],
        out_specs=[vmem] * 4,
        out_shape=(
            jax.ShapeDtypeStruct((1, rows), f32),
            jax.ShapeDtypeStruct((shards, rows), f32),
            jax.ShapeDtypeStruct((blocks // 2, width), f32),
            jax.ShapeDtypeStruct(fixed_values.shape, fixed_values.dtype),
        ),
        scratch_shapes=[pltpu.VMEM((shards, rows), f32), pltpu.SemaphoreType.DMA],
        compiler_params=compiler_params(50),
        name="margins_and_theirs",
    )(returned, fixed, label, slot, fixed_values, block_row)


def mine_kernel(dp_count, residual_ref, values_ref, block_ref, out_ref):
    residual_rows = [residual_ref[i : i + 1, :] for i in range(residual_ref.shape[0])]
    add_blocks(0, dp_count, values_ref, block_ref, residual_rows, out_ref)


def gradient_mine(residual, fixed_values, block_row, blocks, dp_count):
    rows, width = fixed_values.shape

    def kernel(*refs):
        mine_kernel(dp_count, *refs)

    return pl.pallas_call(
        kernel,
        out_shape=jax.ShapeDtypeStruct((blocks // 2, width), f32),
        cost_estimate=pl.CostEstimate(
            flops=2 * rows * blocks * width,
            bytes_accessed=2 * rows * width + 2 * blocks * width,
            transcendentals=0,
        ),
        compiler_params=compiler_params(50),
        name="gradient_mine",
    )(residual, fixed_values, block_row)


def pack_kernel(
    values_ref, feats_in_ref, slot_in_ref, out_ref, start_ref, feats_ref, slot_ref, sem
):
    copies = [
        pltpu.make_async_copy(slot_in_ref, slot_ref, sem.at[0]),
        pltpu.make_async_copy(feats_in_ref, feats_ref, sem.at[1]),
        pltpu.make_async_copy(values_ref.at[pl.ds(0, start_ref.shape[0])], start_ref, sem.at[2]),
    ]
    for copy in copies:
        copy.start()
    copies[0].wait()
    copies[1].wait()
    total = out_ref.shape[0]
    step = min(1024, total)
    for start in range(0, total, step):
        mask = (rows_iota((step, slot_ref.shape[1])) + start) == slot_ref[...]
        one_hot = jnp.where(mask, 1.0, 0.0).astype(bf16)
        out_ref[start : start + step, :] = dot_nn(one_hot, feats_ref[...]).astype(bf16)
    copies[2].wait()


def pack_feats(fixed_values, member_feats, slot_row, slot_total):
    rows, width = member_feats.shape
    vmem = pl.BlockSpec(memory_space=pltpu.VMEM)
    return pl.pallas_call(
        pack_kernel,
        in_specs=[pl.BlockSpec(memory_space=pltpu.HBM)] * 3,
        out_specs=[vmem, vmem],
        out_shape=(
            jax.ShapeDtypeStruct((slot_total, width), bf16),
            jax.ShapeDtypeStruct((rows, fixed_values.shape[1]), bf16),
        ),
        scratch_shapes=[
            pltpu.VMEM((rows, width), bf16),
            pltpu.VMEM((1, rows), jnp.int32),
            pltpu.SemaphoreType.DMA((3,)),
        ],
        cost_estimate=pl.CostEstimate(
            flops=2 * rows * slot_total * width,
            bytes_accessed=2 * rows * width + 2 * slot_total * width,
            transcendentals=0,
        ),
        compiler_params=compiler_params(50),
        name="pack_feats",
    )(fixed_values, member_feats, slot_row)


def message_kernel(pieces, label_ref, slot_ref, fixed_ref, labels_ref, slots_ref, out_ref):
    shards = fixed_ref.shape[0]
    feat = lax.axis_index("feat")
    fixed = pieces[0][:shards, :]
    for piece in pieces[1:]:
        fixed = fixed + piece[:shards, :]
    fixed_ref[...] = fixed
    for k, piece in enumerate(pieces):
        labels_ref[pl.ds(feat ^ k, 1), :] = piece[shards : shards + 1, :]
        slots_ref[pl.ds(feat ^ k, 1), :] = piece[shards + 1 : shards + 2, :]
    destinations, _, capacity = out_ref.shape
    slot = slot_ref[...]
    owner = slot // capacity
    owner_hot = hot(owner, destinations)
    place_hot = jnp.where(hot(slot - owner * capacity, capacity), 1.0, 0.0).astype(bf16)
    score = fixed_ref[pl.ds(feat, 1), :].astype(bf16).astype(f32)
    label = label_ref[...].astype(f32)
    both = jnp.concatenate(
        [jnp.where(owner_hot, score, 0.0), jnp.where(owner_hot, label, 0.0)], axis=0
    )
    placed = dot_nt(both.astype(bf16), place_hot)
    out_ref[:, 0, :] = placed[:destinations]
    out_ref[:, 1, :] = placed[destinations:]


def build_message(pieces, label_row, slot_row, dp_count, capacity):
    rows = slot_row.shape[1]
    shards = len(pieces)

    def kernel(*refs):
        message_kernel(refs[:shards], *refs[shards:])

    return pl.pallas_call(
        kernel,
        out_shape=[jax.ShapeDtypeStruct((shards, rows), f32)] * 3
        + [jax.ShapeDtypeStruct((dp_count, 2, capacity), f32)],
        compiler_params=compiler_params(),
        name="build_message",
    )(*pieces, label_row, slot_row)


def slot_member_kernel(tiles_ref, source_ref, out_ref):
    slots, capacity = out_ref.shape
    source = source_ref[...]
    position = lax.broadcasted_iota(jnp.int32, source.shape, 1) // TILE
    member = jnp.zeros(source.shape, jnp.int32)
    end = jnp.int32(0)
    for m in range(tiles_ref.shape[0]):
        end = end + tiles_ref[m]
        member = member + (position >= end).astype(jnp.int32)
    sender = source // capacity
    sender_hot = jnp.where(hot(sender, slots), member.astype(f32) + 1.0, 0.0).astype(bf16)
    place_hot = jnp.where(hot(source - sender * capacity, capacity), 1.0, 0.0).astype(bf16)
    out_ref[...] = dot_nt(sender_hot, place_hot) - 1.0


def slot_members(member_tiles, source_row, dp_count, capacity):
    return pl.pallas_call(
        slot_member_kernel,
        in_specs=[
            pl.BlockSpec(memory_space=pltpu.SMEM),
            pl.BlockSpec(memory_space=pltpu.VMEM),
        ],
        out_specs=pl.BlockSpec(memory_space=pltpu.VMEM),
        out_shape=jax.ShapeDtypeStruct((dp_count, capacity), f32),
        compiler_params=compiler_params(),
        name="slot_members",
    )(member_tiles, source_row)


def lane_row(pieces):
    lanes = pieces.shape[-1]
    pieces = pieces.reshape(-1, lanes)
    return jnp.concatenate([pieces[i : i + 1] for i in range(pieces.shape[0])], axis=1)


def solve_kernel(feats_ref, message_ref, member_ref, coef_ref, updated_ref, scores_ref):
    feats = feats_ref[...]
    coef = coef_ref[...]
    count = coef.shape[0]
    slots = feats.shape[0]
    lanes = message_ref.shape[2]
    message = message_ref[...]
    sent_score = lane_row(message[:, 0, :])
    label = lane_row(message[:, 1, :])
    own = rows_iota((count, slots)).astype(f32) == lane_row(member_ref[...])

    def pick(vectors):
        high, low = split(vectors, 2)
        both = dot_nt(jnp.concatenate([high, low], axis=0), feats)
        each = both[:count] + both[count:]
        return jnp.sum(jnp.where(own, each, 0.0), axis=0, keepdims=True)

    def spread(row_weights):
        high, low = split(jnp.where(own, row_weights, 0.0), 2)
        return jnp.concatenate([high, low], axis=0)

    def gather(row_weights):
        both = dot_nn(spread(row_weights), feats)
        return both[:count] + both[count:]

    base = pick(coef)
    logits = sent_score + base
    probability = sigmoid(logits)
    weight = probability * (1.0 - probability)
    gradient = gather(label - probability) - ridge_member * coef
    wide = feats.astype(f32)
    square_high, square_low = split(wide * wide, 2)
    weights = spread(weight)
    both = dot_nn(weights, square_high) + dot_nn(weights, square_low)
    diagonal = both[:count] + both[count:] + ridge_member
    step_sum = jnp.zeros_like(coef)
    new_scores = base
    remain = gradient
    scaled = remain / diagonal
    search = scaled
    inner_product = jnp.sum(remain * scaled, axis=1, keepdims=True)
    for iteration in range(CG_ITERS):
        projected = pick(search)
        if iteration + 1 < CG_ITERS:
            image = gather(weight * projected) + ridge_member * search
            curvature = jnp.sum(search * image, axis=1, keepdims=True)
        else:
            row_part = jnp.where(own, weight * projected * projected, 0.0)
            curvature = jnp.sum(row_part, axis=1, keepdims=True) + ridge_member * jnp.sum(
                search * search, axis=1, keepdims=True
            )
        alpha_step = inner_product / curvature
        step_sum = step_sum + alpha_step * search
        row_alpha = jnp.sum(jnp.where(own, alpha_step, 0.0), axis=0, keepdims=True)
        new_scores = new_scores + row_alpha * projected
        if iteration + 1 < CG_ITERS:
            remain = remain - alpha_step * image
            scaled = remain / diagonal
            inner_next = jnp.sum(remain * scaled, axis=1, keepdims=True)
            search = scaled + (inner_next / inner_product) * search
            inner_product = inner_next
    updated_ref[...] = coef + step_sum
    copies = scores_ref.shape[0] * lanes // slots
    for i in range(slots // lanes):
        for copy in range(copies):
            scores_ref[i * copies + copy] = new_scores[:, i * lanes : (i + 1) * lanes]


def solve_members(feats, message, member_slots, member_coef, copies):
    senders, _, capacity = message.shape
    return pl.pallas_call(
        solve_kernel,
        out_shape=(
            jax.ShapeDtypeStruct(member_coef.shape, f32),
            jax.ShapeDtypeStruct((senders * copies, 1, capacity), f32),
        ),
        compiler_params=compiler_params(),
        name="solve_members",
    )(feats, message, member_slots, member_coef)


def swap(value, axis, offset):
    return lax.ppermute(
        value, axis, [(i, i ^ offset) for i in range(lax.axis_size(axis))]
    )


def pick_index(value, index):
    return lax.dynamic_index_in_dim(value, index, 0, keepdims=False)


def exchange(message, side, place, half):
    if half > 4:
        return lax.all_to_all(message, "dp", 0, 0, tiled=True)
    pairs = message.reshape((half, 2) + message.shape[1:])
    own = lax.dynamic_index_in_dim(pairs, side, 1, keepdims=False)
    other = swap(lax.dynamic_index_in_dim(pairs, 1 - side, 1, keepdims=False), "dp", 1)
    both = jnp.where(
        side == 0, jnp.stack([own, other], axis=1), jnp.stack([other, own], axis=1)
    )
    out = jnp.zeros_like(both)
    for k in range(half):
        entry = pick_index(both, place ^ k)
        got = entry if k == 0 else swap(entry, "dp", 2 * k)
        out = lax.dynamic_update_index_in_dim(out, got, place ^ k, 0)
    return out.reshape(message.shape)


def reduce_chunks(theirs, mine, half):
    chunk = mine.shape[0] // half
    sends = theirs.astype(f16)
    if half > 4:
        kept = mine + swap(sends, "dp", 1).astype(f32)
        low = half // 2
        while low:
            got = swap(kept[low * chunk :].astype(f16), "dp", 2 * low)
            kept = kept[: low * chunk] + got.astype(f32)
            low //= 2
        return kept
    kept = [None] * half
    for k in reversed(range(half)):
        at = slice(k * chunk, (k + 1) * chunk)
        kept[k] = mine[at] + swap(sends[at], "dp", 1).astype(f32)
    total = kept[0]
    for k in reversed(range(1, half)):
        total = total + swap(kept[k].astype(f16), "dp", 2 * k).astype(f32)
    return total


def spread_chunks(own, side, place, half, coef):
    rows = own.shape[0]
    out = jnp.zeros(coef.shape, f32)

    def put(out, got, k, parity):
        at = ((place ^ k) * 2 + parity) * rows
        own_coef = lax.dynamic_slice_in_dim(coef, at, rows, 0)
        grad = ridge_fixed * own_coef - got.astype(f32)
        return lax.dynamic_update_slice_in_dim(out, grad, at, 0)

    if half > 4:
        whole = own
        low = 1
        while low < half:
            whole = jnp.concatenate([whole, swap(whole, "dp", 2 * low)])
            low *= 2
        other = swap(whole, "dp", 1)
        for k in range(half):
            at = slice(k * rows, (k + 1) * rows)
            out = put(out, whole[at], k, side)
            out = put(out, other[at], k, 1 - side)
        return out
    same = [own] + [swap(own, "dp", 2 * k) for k in range(1, half)]
    for k in range(half):
        out = put(out, same[k], k, side)
        out = put(out, swap(same[k], "dp", 1), k, 1 - side)
    return out


def body(
    member_feats,
    labels,
    fixed_values,
    fixed_blocks,
    fixed_coef,
    member_coef,
    row_slot,
    tile_source,
    member_tiles,
):
    dp_count = lax.axis_size("dp")
    feat_count = lax.axis_size("feat")
    rows_here = member_feats.shape[0]
    blocks = fixed_coef.shape[0]
    capacity = 2 * rows_here // dp_count
    slot_total = dp_count * capacity
    group_rows = fixed_values.shape[0]
    side = lax.axis_index("dp") % 2
    place = lax.axis_index("dp") // 2
    half = dp_count // 2

    slot_row = row_slot.reshape(1, rows_here)
    label_row = labels.reshape(1, rows_here)
    block_row = fixed_blocks.reshape(1, group_rows)

    send_feats, start = pack_feats(fixed_values, member_feats, slot_row, slot_total)
    got_feats = lax.all_to_all(
        send_feats.reshape(dp_count, capacity, -1), "dp", 0, 0, tiled=True
    ).reshape(slot_total, -1)
    member_slots = slot_members(
        member_tiles, tile_source.reshape(1, -1), dp_count, capacity
    )

    own = partial_scores(
        start, fixed_values, block_row, fixed_coef, label_row, slot_row
    )
    pieces = [own] + [swap(own, "feat", k) for k in range(1, feat_count)]
    fixed, label, slot, message = build_message(
        pieces, label_row, slot_row, dp_count, capacity
    )
    got = exchange(message, side, place, half)

    if capacity % 128:
        got = jnp.moveaxis(got, 1, 0).reshape(1, 2, slot_total)
        member_slots = member_slots.reshape(1, slot_total)
        updated_coef, new_scores = solve_members(got_feats, got, member_slots, member_coef, 1)
        new_scores = jnp.broadcast_to(
            new_scores.reshape(dp_count, 1, 1, capacity), (dp_count, feat_count, 1, capacity)
        ).reshape(dp_count * feat_count, 1, capacity)
    else:
        updated_coef, new_scores = solve_members(
            got_feats, got, member_slots, member_coef, feat_count
        )
    returned = lax.all_to_all(new_scores, ("dp", "feat"), 0, 0, tiled=True)
    margin, residual, theirs, values = margins_and_theirs(
        returned, fixed, label, slot, fixed_values, block_row, blocks, dp_count
    )
    mine = gradient_mine(residual, values, block_row, blocks, dp_count)
    summed = reduce_chunks(theirs, mine, half).astype(f16)
    fixed_grad = spread_chunks(summed, side, place, half, fixed_coef)
    return (margin.reshape(rows_here), updated_coef, fixed_grad)


def solution(mesh):
    placed = (
        P(("dp", "feat"), None),
        P(("dp", "feat")),
        P("dp", "feat"),
        P("dp", "feat"),
        P("feat", None),
        P(("dp", "feat"), None),
        P(("dp", "feat")),
        P(("dp", "feat")),
        P(("dp", "feat")),
    )
    return jax.shard_map(
        body,
        mesh=mesh,
        in_specs=placed,
        out_specs=(P(("dp", "feat")), P(("dp", "feat"), None), P("feat", None)),
        check_vma=False,
    )
```

```python
import jax
import jax.numpy as jnp
from jax import lax
from jax.experimental import pallas as pl
from jax.experimental.pallas import tpu as pltpu
from jax.sharding import PartitionSpec as P

CG_ITERS = 2
TILE = 128

ridge_member = 1.0
ridge_fixed = 1.0
bf16 = jnp.bfloat16
f32 = jnp.float32
f16 = jnp.float16


def split(value, parts):
    out = []
    for _ in range(parts):
        piece = value.astype(bf16)
        out.append(piece)
        value = value - piece.astype(f32)
    return out


def dot_nt(a, b):
    return lax.dot_general(a, b, (((1,), (1,)), ((), ())), preferred_element_type=f32)


def dot_nn(a, b):
    return jnp.dot(a, b, preferred_element_type=f32)


def rows_iota(shape):
    return lax.broadcasted_iota(jnp.int32, shape, 0)


def hot(index, count):
    return rows_iota((count, index.shape[1])) == index


def sigmoid(x):
    return 1.0 / (1.0 + jnp.exp(-x))


def compiler_params(mebibytes=50):
    return pltpu.CompilerParams(vmem_limit_bytes=mebibytes << 20)


def partial_kernel(
    values_ref, block_ref, coef_ref, label_ref, slot_ref, out_ref, held_ref, sem
):
    rows = out_ref.shape[1]
    blocks = coef_ref.shape[0]
    shards = values_ref.shape[0] // rows
    copies = [
        pltpu.make_async_copy(
            values_ref.at[pl.ds(i * rows, rows)], held_ref.at[i], sem.at[i]
        )
        for i in range(shards)
    ]
    for copy in copies:
        copy.start()
    high, low = split(coef_ref[...].T, 2)
    lanes = lax.broadcasted_iota(jnp.int32, (1, TILE), 1)
    out_ref[shards : shards + 1, :] = label_ref[...].astype(f32)
    out_ref[shards + 1 : shards + 2, :] = slot_ref[...].astype(f32)
    for i in range(shards):
        block = block_ref[:, i * rows : (i + 1) * rows]
        column = jnp.broadcast_to(block, (TILE, rows)).T
        copies[i].wait()
        values = held_ref[i]
        product = dot_nn(values, high) + dot_nn(values, low)
        total = jnp.zeros((rows, TILE), f32)
        for at in range(0, blocks, TILE):
            total = total + jnp.where(column == lanes + at, product[:, at : at + TILE], 0.0)
        out_ref[i : i + 1, :] = jnp.sum(total.T, axis=0, keepdims=True)


def partial_scores(fixed_values, block_row, fixed_coef, label_row, slot_row):
    rows, width = fixed_values.shape
    rows_here = slot_row.shape[1]
    blocks = fixed_coef.shape[0]
    shards = rows // rows_here
    vmem = pl.BlockSpec(memory_space=pltpu.VMEM)
    return pl.pallas_call(
        partial_kernel,
        in_specs=[pl.BlockSpec(memory_space=pltpu.HBM)] + [vmem] * 4,
        out_specs=vmem,
        out_shape=jax.ShapeDtypeStruct((shards + 2, rows_here), f32),
        scratch_shapes=[
            pltpu.VMEM((shards, rows_here, width), bf16),
            pltpu.SemaphoreType.DMA((shards,)),
        ],
        cost_estimate=pl.CostEstimate(
            flops=4 * rows * blocks * width,
            bytes_accessed=2 * rows * width + 4 * blocks * width,
            transcendentals=0,
        ),
        compiler_params=compiler_params(50),
        name="partial_scores",
    )(fixed_values, block_row, fixed_coef, label_row, slot_row)


def add_blocks(
    flip, dp_count, shard_values, block_ref, residual_rows, out_ref
):
    kept = out_ref.shape[0]
    chunk = 2 * kept // dp_count
    rows = residual_rows[0].shape[1]
    parity = (lax.axis_index("dp") + flip) % 2
    place = lax.axis_index("dp") // 2
    for i, residual in enumerate(residual_rows):
        block = block_ref[:, i * rows : (i + 1) * rows]
        local = ((block // (2 * chunk)) ^ place) * chunk + block % chunk
        local = jnp.where((block // chunk) % 2 == parity, local, -1)
        mask = hot(local, kept)
        high, low = split(residual, 2)
        left_high = jnp.where(mask, high.astype(f32), 0.0).astype(bf16)
        left_low = jnp.where(mask, low.astype(f32), 0.0).astype(bf16)
        values = shard_values(i)
        total = dot_nn(left_high, values) + dot_nn(left_low, values)
        if i == 0:
            out_ref[...] = total
        else:
            out_ref[...] += total


def margin_kernel(
    dp_count, returned_ref, fixed_ref, label_ref, slot_ref, values_ref, block_ref,
    margin_ref, residual_ref, out_ref, keep_ref, all_ref, held_ref, sem,
):
    kept = keep_ref.shape[0]
    copies = [
        pltpu.make_async_copy(values_ref.at[pl.ds(0, kept)], keep_ref, sem.at[0]),
        pltpu.make_async_copy(
            values_ref.at[pl.ds(kept, held_ref.shape[0])], held_ref, sem.at[1]
        ),
    ]
    for copy in copies:
        copy.start()
    sources, _, capacity = returned_ref.shape
    shards, rows = fixed_ref.shape
    pieces = split(returned_ref[...].reshape(sources, capacity), 3)
    table = jnp.concatenate(pieces, axis=0)
    residual_rows = []
    for i in range(shards):
        slot = slot_ref[i : i + 1, :].astype(jnp.int32)
        owner = slot // capacity
        place_hot = jnp.where(hot(slot - owner * capacity, capacity), 1.0, 0.0).astype(bf16)
        found = dot_nn(table, place_hot)
        found = found[:sources] + (found[sources : 2 * sources] + found[2 * sources :])
        owner_hot = hot(owner * shards + i, sources)
        score = jnp.sum(jnp.where(owner_hot, found, 0.0), axis=0, keepdims=True)
        margin = fixed_ref[i : i + 1, :] + score
        all_ref[i : i + 1, :] = margin
        residual = (label_ref[i : i + 1, :] - sigmoid(margin)) * (1.0 / dp_count)
        residual_ref[i : i + 1, :] = residual
        residual_rows.append(residual)
    margin_ref[...] = all_ref[pl.ds(lax.axis_index("feat"), 1), :]
    for copy in copies:
        copy.wait()

    def shard_values(i):
        if i * rows < kept:
            return keep_ref[i * rows : (i + 1) * rows, :]
        return held_ref[i * rows - kept : (i + 1) * rows - kept, :]

    add_blocks(1, dp_count, shard_values, block_ref, residual_rows, out_ref)


def margins_and_theirs(returned, fixed, label, slot, fixed_values, block_row, blocks, dp_count):
    shards, rows = fixed.shape
    group_rows, width = fixed_values.shape
    kept = rows * (shards // 2)

    def kernel(*refs):
        margin_kernel(dp_count, *refs)

    vmem = pl.BlockSpec(memory_space=pltpu.VMEM)
    return pl.pallas_call(
        kernel,
        in_specs=[vmem] * 4 + [pl.BlockSpec(memory_space=pltpu.HBM), vmem],
        out_specs=[vmem] * 4,
        out_shape=(
            jax.ShapeDtypeStruct((1, rows), f32),
            jax.ShapeDtypeStruct((shards, rows), f32),
            jax.ShapeDtypeStruct((blocks // 2, width), f32),
            jax.ShapeDtypeStruct((kept, width), bf16),
        ),
        scratch_shapes=[
            pltpu.VMEM((shards, rows), f32),
            pltpu.VMEM((group_rows - kept, width), bf16),
            pltpu.SemaphoreType.DMA((2,)),
        ],
        compiler_params=compiler_params(50),
        name="margins_and_theirs",
    )(returned, fixed, label, slot, fixed_values, block_row)


def mine_kernel(
    dp_count, residual_ref, keep_ref, values_ref, block_ref, out_ref, held_ref, sem
):
    shards, rows = residual_ref.shape
    first = keep_ref.shape[0] // rows
    copies = [
        pltpu.make_async_copy(
            values_ref.at[pl.ds(i * rows, rows)], held_ref.at[i - first], sem.at[i - first]
        )
        for i in range(first, shards)
    ]
    for copy in copies:
        copy.start()

    def shard_values(i):
        if i < first:
            return keep_ref[i * rows : (i + 1) * rows, :]
        copies[i - first].wait()
        return held_ref[i - first]

    residual_rows = [residual_ref[i : i + 1, :] for i in range(shards)]
    add_blocks(0, dp_count, shard_values, block_ref, residual_rows, out_ref)


def gradient_mine(residual, keep, fixed_values, block_row, blocks, dp_count):
    rows, width = fixed_values.shape
    shards, rows_here = residual.shape
    copied = shards - keep.shape[0] // rows_here
    vmem = pl.BlockSpec(memory_space=pltpu.VMEM)
    hbm = pl.BlockSpec(memory_space=pltpu.HBM)

    def kernel(*refs):
        mine_kernel(dp_count, *refs)

    return pl.pallas_call(
        kernel,
        in_specs=[vmem, vmem, hbm, vmem],
        out_specs=vmem,
        out_shape=jax.ShapeDtypeStruct((blocks // 2, width), f32),
        scratch_shapes=[
            pltpu.VMEM((copied, rows_here, width), bf16),
            pltpu.SemaphoreType.DMA((copied,)),
        ],
        cost_estimate=pl.CostEstimate(
            flops=2 * rows * blocks * width,
            bytes_accessed=2 * rows * width + 2 * blocks * width,
            transcendentals=0,
        ),
        compiler_params=compiler_params(50),
        name="gradient_mine",
    )(residual, keep, fixed_values, block_row)


def pack_kernel(feats_in_ref, slot_in_ref, out_ref, feats_ref, slot_ref, held_ref, sem):
    loads = [
        pltpu.make_async_copy(slot_in_ref, slot_ref, sem.at[0]),
        pltpu.make_async_copy(feats_in_ref, feats_ref, sem.at[1]),
    ]
    for load in loads:
        load.start()
    for load in loads:
        load.wait()
    pieces, step, _ = held_ref.shape
    stores = []
    for i in range(pieces):
        mask = (rows_iota((step, slot_ref.shape[1])) + i * step) == slot_ref[...]
        one_hot = jnp.where(mask, 1.0, 0.0).astype(bf16)
        held_ref[i] = dot_nn(one_hot, feats_ref[...]).astype(bf16)
        stores.append(
            pltpu.make_async_copy(held_ref.at[i], out_ref.at[pl.ds(i * step, step)], sem.at[2 + i])
        )
        stores[-1].start()
    for store in stores:
        store.wait()


def pack_feats(member_feats, slot_row, slot_total):
    rows, width = member_feats.shape
    step = min(512, slot_total)
    pieces = slot_total // step
    hbm = pl.BlockSpec(memory_space=pltpu.HBM)
    return pl.pallas_call(
        pack_kernel,
        in_specs=[hbm, hbm],
        out_specs=hbm,
        out_shape=jax.ShapeDtypeStruct((slot_total, width), bf16),
        scratch_shapes=[
            pltpu.VMEM((rows, width), bf16),
            pltpu.VMEM((1, rows), jnp.int32),
            pltpu.VMEM((pieces, step, width), bf16),
            pltpu.SemaphoreType.DMA((2 + pieces,)),
        ],
        cost_estimate=pl.CostEstimate(
            flops=2 * rows * slot_total * width,
            bytes_accessed=2 * rows * width + 2 * slot_total * width,
            transcendentals=0,
        ),
        name="pack_feats",
    )(member_feats, slot_row)


def message_kernel(pieces, label_ref, slot_ref, fixed_ref, labels_ref, slots_ref, out_ref):
    shards = fixed_ref.shape[0]
    feat = lax.axis_index("feat")
    fixed = pieces[0][:shards, :]
    for piece in pieces[1:]:
        fixed = fixed + piece[:shards, :]
    fixed_ref[...] = fixed
    for k, piece in enumerate(pieces):
        labels_ref[pl.ds(feat ^ k, 1), :] = piece[shards : shards + 1, :]
        slots_ref[pl.ds(feat ^ k, 1), :] = piece[shards + 1 : shards + 2, :]
    destinations, _, capacity = out_ref.shape
    slot = slot_ref[...]
    owner = slot // capacity
    owner_hot = hot(owner, destinations)
    place_hot = jnp.where(hot(slot - owner * capacity, capacity), 1.0, 0.0).astype(bf16)
    score = fixed_ref[pl.ds(feat, 1), :].astype(bf16).astype(f32)
    label = label_ref[...].astype(f32)
    both = jnp.concatenate(
        [jnp.where(owner_hot, score, 0.0), jnp.where(owner_hot, label, 0.0)], axis=0
    )
    placed = dot_nt(both.astype(bf16), place_hot)
    out_ref[:, 0, :] = placed[:destinations]
    out_ref[:, 1, :] = placed[destinations:]


def build_message(pieces, label_row, slot_row, dp_count, capacity):
    rows = slot_row.shape[1]
    shards = len(pieces)

    def kernel(*refs):
        message_kernel(refs[:shards], *refs[shards:])

    return pl.pallas_call(
        kernel,
        out_shape=[jax.ShapeDtypeStruct((shards, rows), f32)] * 3
        + [jax.ShapeDtypeStruct((dp_count, 2, capacity), f32)],
        compiler_params=compiler_params(),
        name="build_message",
    )(*pieces, label_row, slot_row)


def slot_member_kernel(tiles_ref, source_ref, out_ref):
    slots, capacity = out_ref.shape
    source = source_ref[...]
    position = lax.broadcasted_iota(jnp.int32, source.shape, 1) // TILE
    member = jnp.zeros(source.shape, jnp.int32)
    end = jnp.int32(0)
    for m in range(tiles_ref.shape[0]):
        end = end + tiles_ref[m]
        member = member + (position >= end).astype(jnp.int32)
    sender = source // capacity
    sender_hot = jnp.where(hot(sender, slots), member.astype(f32) + 1.0, 0.0).astype(bf16)
    place_hot = jnp.where(hot(source - sender * capacity, capacity), 1.0, 0.0).astype(bf16)
    out_ref[...] = dot_nt(sender_hot, place_hot) - 1.0


def slot_members(member_tiles, source_row, dp_count, capacity):
    return pl.pallas_call(
        slot_member_kernel,
        in_specs=[
            pl.BlockSpec(memory_space=pltpu.SMEM),
            pl.BlockSpec(memory_space=pltpu.VMEM),
        ],
        out_specs=pl.BlockSpec(memory_space=pltpu.VMEM),
        out_shape=jax.ShapeDtypeStruct((dp_count, capacity), f32),
        compiler_params=compiler_params(),
        name="slot_members",
    )(member_tiles, source_row)


def lane_row(pieces):
    lanes = pieces.shape[-1]
    pieces = pieces.reshape(-1, lanes)
    return jnp.concatenate([pieces[i : i + 1] for i in range(pieces.shape[0])], axis=1)


def solve_kernel(feats_ref, message_ref, member_ref, coef_ref, updated_ref, scores_ref):
    feats = feats_ref[...]
    coef = coef_ref[...]
    count = coef.shape[0]
    slots = feats.shape[0]
    lanes = message_ref.shape[2]
    message = message_ref[...]
    sent_score = lane_row(message[:, 0, :])
    label = lane_row(message[:, 1, :])
    own = rows_iota((count, slots)).astype(f32) == lane_row(member_ref[...])

    def pick(vectors):
        high, low = split(vectors, 2)
        both = dot_nt(jnp.concatenate([high, low], axis=0), feats)
        each = both[:count] + both[count:]
        return jnp.sum(jnp.where(own, each, 0.0), axis=0, keepdims=True)

    def spread(row_weights):
        high, low = split(jnp.where(own, row_weights, 0.0), 2)
        return jnp.concatenate([high, low], axis=0)

    def gather(row_weights):
        both = dot_nn(spread(row_weights), feats)
        return both[:count] + both[count:]

    base = pick(coef)
    logits = sent_score + base
    probability = sigmoid(logits)
    weight = probability * (1.0 - probability)
    gradient = gather(label - probability) - ridge_member * coef
    wide = feats.astype(f32)
    square_high, square_low = split(wide * wide, 2)
    weights = spread(weight)
    both = dot_nn(weights, square_high) + dot_nn(weights, square_low)
    diagonal = both[:count] + both[count:] + ridge_member
    step_sum = jnp.zeros_like(coef)
    new_scores = base
    remain = gradient
    scaled = remain / diagonal
    search = scaled
    inner_product = jnp.sum(remain * scaled, axis=1, keepdims=True)
    for iteration in range(CG_ITERS):
        projected = pick(search)
        if iteration + 1 < CG_ITERS:
            image = gather(weight * projected) + ridge_member * search
            curvature = jnp.sum(search * image, axis=1, keepdims=True)
        else:
            row_part = jnp.where(own, weight * projected * projected, 0.0)
            curvature = jnp.sum(row_part, axis=1, keepdims=True) + ridge_member * jnp.sum(
                search * search, axis=1, keepdims=True
            )
        alpha_step = inner_product / curvature
        step_sum = step_sum + alpha_step * search
        row_alpha = jnp.sum(jnp.where(own, alpha_step, 0.0), axis=0, keepdims=True)
        new_scores = new_scores + row_alpha * projected
        if iteration + 1 < CG_ITERS:
            remain = remain - alpha_step * image
            scaled = remain / diagonal
            inner_next = jnp.sum(remain * scaled, axis=1, keepdims=True)
            search = scaled + (inner_next / inner_product) * search
            inner_product = inner_next
    updated_ref[...] = coef + step_sum
    copies = scores_ref.shape[0] * lanes // slots
    for i in range(slots // lanes):
        for copy in range(copies):
            scores_ref[i * copies + copy] = new_scores[:, i * lanes : (i + 1) * lanes]


def solve_members(feats, message, member_slots, member_coef, copies):
    senders, _, capacity = message.shape
    return pl.pallas_call(
        solve_kernel,
        out_shape=(
            jax.ShapeDtypeStruct(member_coef.shape, f32),
            jax.ShapeDtypeStruct((senders * copies, 1, capacity), f32),
        ),
        compiler_params=compiler_params(),
        name="solve_members",
    )(feats, message, member_slots, member_coef)


def swap(value, axis, offset):
    return lax.ppermute(
        value, axis, [(i, i ^ offset) for i in range(lax.axis_size(axis))]
    )


def pick_index(value, index):
    return lax.dynamic_index_in_dim(value, index, 0, keepdims=False)


def exchange(message, side, place, half):
    if half > 4:
        return lax.all_to_all(message, "dp", 0, 0, tiled=True)
    pairs = message.reshape((half, 2) + message.shape[1:])
    own = lax.dynamic_index_in_dim(pairs, side, 1, keepdims=False)
    other = swap(lax.dynamic_index_in_dim(pairs, 1 - side, 1, keepdims=False), "dp", 1)
    both = jnp.where(
        side == 0, jnp.stack([own, other], axis=1), jnp.stack([other, own], axis=1)
    )
    out = jnp.zeros_like(both)
    for k in range(half):
        entry = pick_index(both, place ^ k)
        got = entry if k == 0 else swap(entry, "dp", 2 * k)
        out = lax.dynamic_update_index_in_dim(out, got, place ^ k, 0)
    return out.reshape(message.shape)


def reduce_chunks(theirs, mine, half):
    chunk = mine.shape[0] // half
    sends = theirs.astype(f16)
    if half > 4:
        kept = mine + swap(sends, "dp", 1).astype(f32)
        low = half // 2
        while low:
            got = swap(kept[low * chunk :].astype(f16), "dp", 2 * low)
            kept = kept[: low * chunk] + got.astype(f32)
            low //= 2
        return kept
    order = [k for k in (1, 3, 2, 0) if k < half]
    got = {}
    for k in order:
        got[k] = swap(sends[k * chunk : (k + 1) * chunk], "dp", 1)
    landed = []
    before = None
    for k in order:
        other = got[k]
        if before is not None:
            other = lax.optimization_barrier((other, before))[0]
        kept = mine[k * chunk : (k + 1) * chunk] + other.astype(f32)
        if k == 0:
            total = kept
        else:
            before = kept.astype(f16)
            landed.append(swap(before, "dp", 2 * k))
    for piece in landed:
        total = total + piece.astype(f32)
    return total


def spread_chunks(own, side, place, half, coef):
    rows = own.shape[0]
    out = jnp.zeros(coef.shape, f32)

    def put(out, got, k, parity):
        at = ((place ^ k) * 2 + parity) * rows
        own_coef = lax.dynamic_slice_in_dim(coef, at, rows, 0)
        grad = ridge_fixed * own_coef - got.astype(f32)
        return lax.dynamic_update_slice_in_dim(out, grad, at, 0)

    if half > 4:
        whole = own
        low = 1
        while low < half:
            whole = jnp.concatenate([whole, swap(whole, "dp", 2 * low)])
            low *= 2
        other = swap(whole, "dp", 1)
        for k in range(half):
            at = slice(k * rows, (k + 1) * rows)
            out = put(out, whole[at], k, side)
            out = put(out, other[at], k, 1 - side)
        return out
    same = {0: own}
    for k in (1, 3, 2):
        same[k] = swap(own, "dp", 2 * k)
    for k in (0,) + (1, 3, 2):
        other = swap(same[k], "dp", 1)
        pair = jnp.where(
            side == 0,
            jnp.concatenate([same[k], other]),
            jnp.concatenate([other, same[k]]),
        )
        at = (place ^ k) * 2 * rows
        own_coef = lax.dynamic_slice_in_dim(coef, at, 2 * rows, 0)
        grad = ridge_fixed * own_coef - pair.astype(f32)
        out = lax.dynamic_update_slice_in_dim(out, grad, at, 0)
    return out


def body(
    member_feats,
    labels,
    fixed_values,
    fixed_blocks,
    fixed_coef,
    member_coef,
    row_slot,
    tile_source,
    member_tiles,
):
    dp_count = lax.axis_size("dp")
    feat_count = lax.axis_size("feat")
    rows_here = member_feats.shape[0]
    blocks = fixed_coef.shape[0]
    capacity = 2 * rows_here // dp_count
    slot_total = dp_count * capacity
    group_rows = fixed_values.shape[0]
    side = lax.axis_index("dp") % 2
    place = lax.axis_index("dp") // 2
    half = dp_count // 2

    slot_row = row_slot.reshape(1, rows_here)
    label_row = labels.reshape(1, rows_here)
    block_row = fixed_blocks.reshape(1, group_rows)

    send_feats = pack_feats(member_feats, slot_row, slot_total)
    got_feats = lax.all_to_all(
        send_feats.reshape(dp_count, capacity, -1), "dp", 0, 0, tiled=True
    ).reshape(slot_total, -1)
    member_slots = slot_members(
        member_tiles, tile_source.reshape(1, -1), dp_count, capacity
    )

    own = partial_scores(fixed_values, block_row, fixed_coef, label_row, slot_row)
    pieces = [own] + [swap(own, "feat", k) for k in range(1, feat_count)]
    fixed, label, slot, message = build_message(
        pieces, label_row, slot_row, dp_count, capacity
    )
    got = exchange(message, side, place, half)

    if capacity % 128:
        got = jnp.moveaxis(got, 1, 0).reshape(1, 2, slot_total)
        member_slots = member_slots.reshape(1, slot_total)
        updated_coef, new_scores = solve_members(got_feats, got, member_slots, member_coef, 1)
        new_scores = jnp.broadcast_to(
            new_scores.reshape(dp_count, 1, 1, capacity), (dp_count, feat_count, 1, capacity)
        ).reshape(dp_count * feat_count, 1, capacity)
    else:
        updated_coef, new_scores = solve_members(
            got_feats, got, member_slots, member_coef, feat_count
        )
    returned = lax.all_to_all(new_scores, ("dp", "feat"), 0, 0, tiled=True)
    margin, residual, theirs, keep = margins_and_theirs(
        returned, fixed, label, slot, fixed_values, block_row, blocks, dp_count
    )
    mine = gradient_mine(
        residual, keep, fixed_values, block_row, blocks, dp_count
    )
    summed = reduce_chunks(theirs, mine, half).astype(f16)
    fixed_grad = spread_chunks(summed, side, place, half, fixed_coef)
    return (margin.reshape(rows_here), updated_coef, fixed_grad)


def solution(mesh):
    placed = (
        P(("dp", "feat"), None),
        P(("dp", "feat")),
        P("dp", "feat"),
        P("dp", "feat"),
        P("feat", None),
        P(("dp", "feat"), None),
        P(("dp", "feat")),
        P(("dp", "feat")),
        P(("dp", "feat")),
    )
    return jax.shard_map(
        body,
        mesh=mesh,
        in_specs=placed,
        out_specs=(P(("dp", "feat")), P(("dp", "feat"), None), P("feat", None)),
        check_vma=False,
    )
```

```python
import jax
import jax.numpy as jnp
from jax import lax
from jax.experimental import pallas as pl
from jax.experimental.pallas import tpu as pltpu
from jax.sharding import PartitionSpec as P

CG_ITERS = 2
TILE = 128

ridge_member = 1.0
ridge_fixed = 1.0
bf16 = jnp.bfloat16
f32 = jnp.float32
f16 = jnp.float16


def split(value, parts):
    out = []
    for _ in range(parts):
        piece = value.astype(bf16)
        out.append(piece)
        value = value - piece.astype(f32)
    return out


def dot_nt(a, b):
    return lax.dot_general(a, b, (((1,), (1,)), ((), ())), preferred_element_type=f32)


def dot_nn(a, b):
    return jnp.dot(a, b, preferred_element_type=f32)


def rows_iota(shape):
    return lax.broadcasted_iota(jnp.int32, shape, 0)


def hot(index, count):
    return rows_iota((count, index.shape[1])) == index


def sigmoid(x):
    return 1.0 / (1.0 + jnp.exp(-x))


def compiler_params(mebibytes=50):
    return pltpu.CompilerParams(vmem_limit_bytes=mebibytes << 20)


def partial_kernel(
    values_ref, block_ref, coef_ref, label_ref, slot_ref, out_ref, keep_ref, held_ref, sem
):
    rows = out_ref.shape[1]
    blocks = coef_ref.shape[0]
    shards = values_ref.shape[0] // rows
    first = keep_ref.shape[0] // rows
    copies = [
        pltpu.make_async_copy(
            values_ref.at[pl.ds(i * rows, rows)],
            keep_ref.at[pl.ds(i * rows, rows)] if i < first else held_ref.at[i - first],
            sem.at[i],
        )
        for i in range(shards)
    ]
    for copy in copies:
        copy.start()
    high, low = split(coef_ref[...].T, 2)
    lanes = lax.broadcasted_iota(jnp.int32, (1, TILE), 1)
    out_ref[shards : shards + 1, :] = label_ref[...].astype(f32)
    out_ref[shards + 1 : shards + 2, :] = slot_ref[...].astype(f32)
    for i in range(shards):
        block = block_ref[:, i * rows : (i + 1) * rows]
        column = jnp.broadcast_to(block, (TILE, rows)).T
        copies[i].wait()
        values = keep_ref[i * rows : (i + 1) * rows, :] if i < first else held_ref[i - first]
        product = dot_nn(values, high) + dot_nn(values, low)
        total = jnp.zeros((rows, TILE), f32)
        for at in range(0, blocks, TILE):
            total = total + jnp.where(column == lanes + at, product[:, at : at + TILE], 0.0)
        out_ref[i : i + 1, :] = jnp.sum(total.T, axis=0, keepdims=True)


def partial_scores(fixed_values, block_row, fixed_coef, label_row, slot_row):
    rows, width = fixed_values.shape
    rows_here = slot_row.shape[1]
    blocks = fixed_coef.shape[0]
    shards = rows // rows_here
    first = shards // 2
    vmem = pl.BlockSpec(memory_space=pltpu.VMEM)
    return pl.pallas_call(
        partial_kernel,
        in_specs=[pl.BlockSpec(memory_space=pltpu.HBM)] + [vmem] * 4,
        out_specs=[vmem, vmem],
        out_shape=(
            jax.ShapeDtypeStruct((shards + 2, rows_here), f32),
            jax.ShapeDtypeStruct((first * rows_here, width), bf16),
        ),
        scratch_shapes=[
            pltpu.VMEM((shards - first, rows_here, width), bf16),
            pltpu.SemaphoreType.DMA((shards,)),
        ],
        cost_estimate=pl.CostEstimate(
            flops=4 * rows * blocks * width,
            bytes_accessed=2 * rows * width + 4 * blocks * width,
            transcendentals=0,
        ),
        compiler_params=compiler_params(50),
        name="partial_scores",
    )(fixed_values, block_row, fixed_coef, label_row, slot_row)


def add_blocks(
    flip, dp_count, shard_values, block_ref, residual_rows, out_ref
):
    kept = out_ref.shape[0]
    chunk = 2 * kept // dp_count
    rows = residual_rows[0].shape[1]
    parity = (lax.axis_index("dp") + flip) % 2
    place = lax.axis_index("dp") // 2
    for i, residual in enumerate(residual_rows):
        block = block_ref[:, i * rows : (i + 1) * rows]
        local = ((block // (2 * chunk)) ^ place) * chunk + block % chunk
        local = jnp.where((block // chunk) % 2 == parity, local, -1)
        mask = hot(local, kept)
        high, low = split(residual, 2)
        left_high = jnp.where(mask, high.astype(f32), 0.0).astype(bf16)
        left_low = jnp.where(mask, low.astype(f32), 0.0).astype(bf16)
        values = shard_values(i)
        total = dot_nn(left_high, values) + dot_nn(left_low, values)
        if i == 0:
            out_ref[...] = total
        else:
            out_ref[...] += total


def lookup_products(returned_ref, slot, shards, shard):
    sources, _, capacity = returned_ref.shape
    table = jnp.concatenate(split(returned_ref[...].reshape(sources, capacity), 3), axis=0)
    owner = slot // capacity
    place_hot = jnp.where(hot(slot - owner * capacity, capacity), 1.0, 0.0).astype(bf16)
    found = dot_nn(table, place_hot)
    found = found[:sources] + (found[sources : 2 * sources] + found[2 * sources :])
    owner_hot = hot(owner * shards + shard, sources)
    return jnp.sum(jnp.where(owner_hot, found, 0.0), axis=0, keepdims=True)


def lookup_lanes(returned_ref, slot, shards, shard):
    sources, _, capacity = returned_ref.shape
    rows = slot.shape[1]
    folds = rows // TILE
    slot = jnp.concatenate([slot[:, i * TILE : (i + 1) * TILE] for i in range(folds)], axis=0)
    block = slot // TILE
    lane = slot % TILE
    score = jnp.zeros(slot.shape, f32)
    per_owner = capacity // TILE
    for owner in range(sources // shards):
        for part in range(per_owner):
            piece = returned_ref[owner * shards + shard, :, part * TILE : (part + 1) * TILE]
            spread = jnp.broadcast_to(piece, slot.shape)
            found = jnp.take_along_axis(spread, lane, axis=1)
            score = jnp.where(block == owner * per_owner + part, found, score)
    return jnp.concatenate([score[i : i + 1] for i in range(folds)], axis=1)


def margin_kernel(
    dp_count, returned_ref, fixed_ref, label_ref, slot_ref, keep_ref, values_ref, block_ref,
    margin_ref, residual_ref, out_ref, all_ref, held_ref, sem,
):
    kept = keep_ref.shape[0]
    copy = pltpu.make_async_copy(values_ref.at[pl.ds(kept, held_ref.shape[0])], held_ref, sem)
    copy.start()
    capacity = returned_ref.shape[2]
    shards, rows = fixed_ref.shape
    lookup = lookup_lanes if capacity % TILE == 0 else lookup_products
    residual_rows = []
    for i in range(shards):
        slot = slot_ref[i : i + 1, :].astype(jnp.int32)
        score = lookup(returned_ref, slot, shards, i)
        margin = fixed_ref[i : i + 1, :] + score
        all_ref[i : i + 1, :] = margin
        residual = (label_ref[i : i + 1, :] - sigmoid(margin)) * (1.0 / dp_count)
        residual_ref[i : i + 1, :] = residual
        residual_rows.append(residual)
    margin_ref[...] = all_ref[pl.ds(lax.axis_index("feat"), 1), :]

    def shard_values(i):
        if i * rows == kept:
            copy.wait()
        if i * rows < kept:
            return keep_ref[i * rows : (i + 1) * rows, :]
        return held_ref[i * rows - kept : (i + 1) * rows - kept, :]

    add_blocks(1, dp_count, shard_values, block_ref, residual_rows, out_ref)


def margins_and_theirs(
    returned, fixed, label, slot, keep, fixed_values, block_row, blocks, dp_count
):
    shards, rows = fixed.shape
    group_rows, width = fixed_values.shape
    kept = keep.shape[0]

    def kernel(*refs):
        margin_kernel(dp_count, *refs)

    vmem = pl.BlockSpec(memory_space=pltpu.VMEM)
    return pl.pallas_call(
        kernel,
        in_specs=[vmem] * 5 + [pl.BlockSpec(memory_space=pltpu.HBM), vmem],
        out_specs=[vmem] * 3,
        out_shape=(
            jax.ShapeDtypeStruct((1, rows), f32),
            jax.ShapeDtypeStruct((shards, rows), f32),
            jax.ShapeDtypeStruct((blocks // 2, width), f32),
        ),
        scratch_shapes=[
            pltpu.VMEM((shards, rows), f32),
            pltpu.VMEM((group_rows - kept, width), bf16),
            pltpu.SemaphoreType.DMA,
        ],
        compiler_params=compiler_params(50),
        name="margins_and_theirs",
    )(returned, fixed, label, slot, keep, fixed_values, block_row)


def mine_kernel(
    dp_count, residual_ref, keep_ref, values_ref, block_ref, out_ref, held_ref, sem
):
    shards, rows = residual_ref.shape
    first = keep_ref.shape[0] // rows
    copies = [
        pltpu.make_async_copy(
            values_ref.at[pl.ds(i * rows, rows)], held_ref.at[i - first], sem.at[i - first]
        )
        for i in range(first, shards)
    ]
    for copy in copies:
        copy.start()

    def shard_values(i):
        if i < first:
            return keep_ref[i * rows : (i + 1) * rows, :]
        copies[i - first].wait()
        return held_ref[i - first]

    residual_rows = [residual_ref[i : i + 1, :] for i in range(shards)]
    add_blocks(0, dp_count, shard_values, block_ref, residual_rows, out_ref)


def gradient_mine(residual, keep, fixed_values, block_row, blocks, dp_count):
    rows, width = fixed_values.shape
    shards, rows_here = residual.shape
    copied = shards - keep.shape[0] // rows_here
    vmem = pl.BlockSpec(memory_space=pltpu.VMEM)
    hbm = pl.BlockSpec(memory_space=pltpu.HBM)

    def kernel(*refs):
        mine_kernel(dp_count, *refs)

    return pl.pallas_call(
        kernel,
        in_specs=[vmem, vmem, hbm, vmem],
        out_specs=vmem,
        out_shape=jax.ShapeDtypeStruct((blocks // 2, width), f32),
        scratch_shapes=[
            pltpu.VMEM((copied, rows_here, width), bf16),
            pltpu.SemaphoreType.DMA((copied,)),
        ],
        cost_estimate=pl.CostEstimate(
            flops=2 * rows * blocks * width,
            bytes_accessed=2 * rows * width + 2 * blocks * width,
            transcendentals=0,
        ),
        compiler_params=compiler_params(50),
        name="gradient_mine",
    )(residual, keep, fixed_values, block_row)


def pack_kernel(feats_in_ref, slot_in_ref, out_ref, feats_ref, slot_ref, held_ref, sem):
    loads = [
        pltpu.make_async_copy(slot_in_ref, slot_ref, sem.at[0]),
        pltpu.make_async_copy(feats_in_ref, feats_ref, sem.at[1]),
    ]
    for load in loads:
        load.start()
    for load in loads:
        load.wait()
    pieces, step, _ = held_ref.shape
    stores = []
    for i in range(pieces):
        mask = (rows_iota((step, slot_ref.shape[1])) + i * step) == slot_ref[...]
        one_hot = jnp.where(mask, 1.0, 0.0).astype(bf16)
        held_ref[i] = dot_nn(one_hot, feats_ref[...]).astype(bf16)
        stores.append(
            pltpu.make_async_copy(held_ref.at[i], out_ref.at[pl.ds(i * step, step)], sem.at[2 + i])
        )
        stores[-1].start()
    for store in stores:
        store.wait()


def pack_feats(member_feats, slot_row, slot_total):
    rows, width = member_feats.shape
    step = min(512, slot_total)
    pieces = slot_total // step
    hbm = pl.BlockSpec(memory_space=pltpu.HBM)
    return pl.pallas_call(
        pack_kernel,
        in_specs=[hbm, hbm],
        out_specs=hbm,
        out_shape=jax.ShapeDtypeStruct((slot_total, width), bf16),
        scratch_shapes=[
            pltpu.VMEM((rows, width), bf16),
            pltpu.VMEM((1, rows), jnp.int32),
            pltpu.VMEM((pieces, step, width), bf16),
            pltpu.SemaphoreType.DMA((2 + pieces,)),
        ],
        cost_estimate=pl.CostEstimate(
            flops=2 * rows * slot_total * width,
            bytes_accessed=2 * rows * width + 2 * slot_total * width,
            transcendentals=0,
        ),
        name="pack_feats",
    )(member_feats, slot_row)


def message_kernel(pieces, label_ref, slot_ref, fixed_ref, labels_ref, slots_ref, out_ref):
    shards = fixed_ref.shape[0]
    feat = lax.axis_index("feat")
    fixed = pieces[0][:shards, :]
    for piece in pieces[1:]:
        fixed = fixed + piece[:shards, :]
    fixed_ref[...] = fixed
    for k, piece in enumerate(pieces):
        labels_ref[pl.ds(feat ^ k, 1), :] = piece[shards : shards + 1, :]
        slots_ref[pl.ds(feat ^ k, 1), :] = piece[shards + 1 : shards + 2, :]
    destinations, _, capacity = out_ref.shape
    slot = slot_ref[...]
    owner = slot // capacity
    owner_hot = hot(owner, destinations)
    place_hot = jnp.where(hot(slot - owner * capacity, capacity), 1.0, 0.0).astype(bf16)
    score = fixed_ref[pl.ds(feat, 1), :].astype(bf16).astype(f32)
    label = label_ref[...].astype(f32)
    both = jnp.concatenate(
        [jnp.where(owner_hot, score, 0.0), jnp.where(owner_hot, label, 0.0)], axis=0
    )
    placed = dot_nt(both.astype(bf16), place_hot)
    out_ref[:, 0, :] = placed[:destinations]
    out_ref[:, 1, :] = placed[destinations:]


def build_message(pieces, label_row, slot_row, dp_count, capacity):
    rows = slot_row.shape[1]
    shards = len(pieces)

    def kernel(*refs):
        message_kernel(refs[:shards], *refs[shards:])

    return pl.pallas_call(
        kernel,
        out_shape=[jax.ShapeDtypeStruct((shards, rows), f32)] * 3
        + [jax.ShapeDtypeStruct((dp_count, 2, capacity), f32)],
        compiler_params=compiler_params(),
        name="build_message",
    )(*pieces, label_row, slot_row)


def slot_member_kernel(tiles_ref, source_ref, out_ref):
    slots, capacity = out_ref.shape
    source = source_ref[...]
    position = lax.broadcasted_iota(jnp.int32, source.shape, 1) // TILE
    member = jnp.zeros(source.shape, jnp.int32)
    end = jnp.int32(0)
    for m in range(tiles_ref.shape[0]):
        end = end + tiles_ref[m]
        member = member + (position >= end).astype(jnp.int32)
    sender = source // capacity
    sender_hot = jnp.where(hot(sender, slots), member.astype(f32) + 1.0, 0.0).astype(bf16)
    place_hot = jnp.where(hot(source - sender * capacity, capacity), 1.0, 0.0).astype(bf16)
    out_ref[...] = dot_nt(sender_hot, place_hot) - 1.0


def slot_members(member_tiles, source_row, dp_count, capacity):
    return pl.pallas_call(
        slot_member_kernel,
        in_specs=[
            pl.BlockSpec(memory_space=pltpu.SMEM),
            pl.BlockSpec(memory_space=pltpu.VMEM),
        ],
        out_specs=pl.BlockSpec(memory_space=pltpu.VMEM),
        out_shape=jax.ShapeDtypeStruct((dp_count, capacity), f32),
        compiler_params=compiler_params(),
        name="slot_members",
    )(member_tiles, source_row)


def lane_row(pieces):
    lanes = pieces.shape[-1]
    pieces = pieces.reshape(-1, lanes)
    return jnp.concatenate([pieces[i : i + 1] for i in range(pieces.shape[0])], axis=1)


def solve_kernel(feats_ref, message_ref, member_ref, coef_ref, updated_ref, scores_ref):
    feats = feats_ref[...]
    coef = coef_ref[...]
    count = coef.shape[0]
    slots = feats.shape[0]
    lanes = message_ref.shape[2]
    message = message_ref[...]
    sent_score = lane_row(message[:, 0, :])
    label = lane_row(message[:, 1, :])
    own = rows_iota((count, slots)).astype(f32) == lane_row(member_ref[...])

    def pick(vectors):
        high, low = split(vectors, 2)
        both = dot_nt(jnp.concatenate([high, low], axis=0), feats)
        each = both[:count] + both[count:]
        return jnp.sum(jnp.where(own, each, 0.0), axis=0, keepdims=True)

    def spread(row_weights):
        high, low = split(jnp.where(own, row_weights, 0.0), 2)
        return jnp.concatenate([high, low], axis=0)

    def gather(row_weights):
        both = dot_nn(spread(row_weights), feats)
        return both[:count] + both[count:]

    base = pick(coef)
    logits = sent_score + base
    probability = sigmoid(logits)
    weight = probability * (1.0 - probability)
    gradient = gather(label - probability) - ridge_member * coef
    wide = feats.astype(f32)
    square_high, square_low = split(wide * wide, 2)
    weights = spread(weight)
    both = dot_nn(weights, square_high) + dot_nn(weights, square_low)
    diagonal = both[:count] + both[count:] + ridge_member
    step_sum = jnp.zeros_like(coef)
    new_scores = base
    remain = gradient
    scaled = remain / diagonal
    search = scaled
    inner_product = jnp.sum(remain * scaled, axis=1, keepdims=True)
    for iteration in range(CG_ITERS):
        projected = pick(search)
        if iteration + 1 < CG_ITERS:
            image = gather(weight * projected) + ridge_member * search
            curvature = jnp.sum(search * image, axis=1, keepdims=True)
        else:
            row_part = jnp.where(own, weight * projected * projected, 0.0)
            curvature = jnp.sum(row_part, axis=1, keepdims=True) + ridge_member * jnp.sum(
                search * search, axis=1, keepdims=True
            )
        alpha_step = inner_product / curvature
        step_sum = step_sum + alpha_step * search
        row_alpha = jnp.sum(jnp.where(own, alpha_step, 0.0), axis=0, keepdims=True)
        new_scores = new_scores + row_alpha * projected
        if iteration + 1 < CG_ITERS:
            remain = remain - alpha_step * image
            scaled = remain / diagonal
            inner_next = jnp.sum(remain * scaled, axis=1, keepdims=True)
            search = scaled + (inner_next / inner_product) * search
            inner_product = inner_next
    updated_ref[...] = coef + step_sum
    copies = scores_ref.shape[0] * lanes // slots
    for i in range(slots // lanes):
        for copy in range(copies):
            scores_ref[i * copies + copy] = new_scores[:, i * lanes : (i + 1) * lanes]


def solve_members(feats, message, member_slots, member_coef, copies):
    senders, _, capacity = message.shape
    return pl.pallas_call(
        solve_kernel,
        out_shape=(
            jax.ShapeDtypeStruct(member_coef.shape, f32),
            jax.ShapeDtypeStruct((senders * copies, 1, capacity), f32),
        ),
        compiler_params=compiler_params(),
        name="solve_members",
    )(feats, message, member_slots, member_coef)


def swap(value, axis, offset):
    return lax.ppermute(
        value, axis, [(i, i ^ offset) for i in range(lax.axis_size(axis))]
    )


def pick_index(value, index):
    return lax.dynamic_index_in_dim(value, index, 0, keepdims=False)


def exchange(message, side, place, half):
    if half > 4:
        return lax.all_to_all(message, "dp", 0, 0, tiled=True)
    pairs = message.reshape((half, 2) + message.shape[1:])
    own = lax.dynamic_index_in_dim(pairs, side, 1, keepdims=False)
    other = swap(lax.dynamic_index_in_dim(pairs, 1 - side, 1, keepdims=False), "dp", 1)
    both = jnp.where(
        side == 0, jnp.stack([own, other], axis=1), jnp.stack([other, own], axis=1)
    )
    out = jnp.zeros_like(both)
    for k in range(half):
        entry = pick_index(both, place ^ k)
        got = entry if k == 0 else swap(entry, "dp", 2 * k)
        out = lax.dynamic_update_index_in_dim(out, got, place ^ k, 0)
    return out.reshape(message.shape)


def reduce_chunks(theirs, mine, half):
    chunk = mine.shape[0] // half
    sends = theirs.astype(f16)
    if half > 4:
        kept = mine + swap(sends, "dp", 1).astype(f32)
        low = half // 2
        while low:
            got = swap(kept[low * chunk :].astype(f16), "dp", 2 * low)
            kept = kept[: low * chunk] + got.astype(f32)
            low //= 2
        return kept
    order = [k for k in (1, 3, 2, 0) if k < half]
    got = {}
    for k in order:
        got[k] = swap(sends[k * chunk : (k + 1) * chunk], "dp", 1)
    landed = []
    before = None
    for k in order:
        other = got[k]
        if before is not None:
            other = lax.optimization_barrier((other, before))[0]
        kept = mine[k * chunk : (k + 1) * chunk] + other.astype(f32)
        if k == 0:
            total = kept
        else:
            before = kept.astype(f16)
            landed.append(swap(before, "dp", 2 * k))
    for piece in landed:
        total = total + piece.astype(f32)
    return total


def spread_chunks(own, side, place, half, coef):
    rows = own.shape[0]
    out = jnp.zeros(coef.shape, f32)

    def put(out, got, k, parity):
        at = ((place ^ k) * 2 + parity) * rows
        own_coef = lax.dynamic_slice_in_dim(coef, at, rows, 0)
        grad = ridge_fixed * own_coef - got.astype(f32)
        return lax.dynamic_update_slice_in_dim(out, grad, at, 0)

    if half > 4:
        whole = own
        low = 1
        while low < half:
            whole = jnp.concatenate([whole, swap(whole, "dp", 2 * low)])
            low *= 2
        other = swap(whole, "dp", 1)
        for k in range(half):
            at = slice(k * rows, (k + 1) * rows)
            out = put(out, whole[at], k, side)
            out = put(out, other[at], k, 1 - side)
        return out
    same = {0: own}
    for k in (1, 3, 2):
        same[k] = swap(own, "dp", 2 * k)
    for k in (0,) + (1, 3, 2):
        other = swap(same[k], "dp", 1)
        pair = jnp.where(
            side == 0,
            jnp.concatenate([same[k], other]),
            jnp.concatenate([other, same[k]]),
        )
        at = (place ^ k) * 2 * rows
        own_coef = lax.dynamic_slice_in_dim(coef, at, 2 * rows, 0)
        grad = ridge_fixed * own_coef - pair.astype(f32)
        out = lax.dynamic_update_slice_in_dim(out, grad, at, 0)
    return out


def body(
    member_feats,
    labels,
    fixed_values,
    fixed_blocks,
    fixed_coef,
    member_coef,
    row_slot,
    tile_source,
    member_tiles,
):
    dp_count = lax.axis_size("dp")
    feat_count = lax.axis_size("feat")
    rows_here = member_feats.shape[0]
    blocks = fixed_coef.shape[0]
    capacity = 2 * rows_here // dp_count
    slot_total = dp_count * capacity
    group_rows = fixed_values.shape[0]
    side = lax.axis_index("dp") % 2
    place = lax.axis_index("dp") // 2
    half = dp_count // 2

    slot_row = row_slot.reshape(1, rows_here)
    label_row = labels.reshape(1, rows_here)
    block_row = fixed_blocks.reshape(1, group_rows)

    send_feats = pack_feats(member_feats, slot_row, slot_total)
    got_feats = lax.all_to_all(
        send_feats.reshape(dp_count, capacity, -1), "dp", 0, 0, tiled=True
    ).reshape(slot_total, -1)
    member_slots = slot_members(
        member_tiles, tile_source.reshape(1, -1), dp_count, capacity
    )

    own, keep = partial_scores(fixed_values, block_row, fixed_coef, label_row, slot_row)
    pieces = [own] + [swap(own, "feat", k) for k in range(1, feat_count)]
    fixed, label, slot, message = build_message(
        pieces, label_row, slot_row, dp_count, capacity
    )
    got = exchange(message, side, place, half)

    if capacity % 128:
        got = jnp.moveaxis(got, 1, 0).reshape(1, 2, slot_total)
        member_slots = member_slots.reshape(1, slot_total)
        updated_coef, new_scores = solve_members(got_feats, got, member_slots, member_coef, 1)
        new_scores = jnp.broadcast_to(
            new_scores.reshape(dp_count, 1, 1, capacity), (dp_count, feat_count, 1, capacity)
        ).reshape(dp_count * feat_count, 1, capacity)
    else:
        updated_coef, new_scores = solve_members(
            got_feats, got, member_slots, member_coef, feat_count
        )
    returned = lax.all_to_all(new_scores, ("dp", "feat"), 0, 0, tiled=True)
    margin, residual, theirs = margins_and_theirs(
        returned, fixed, label, slot, keep, fixed_values, block_row, blocks, dp_count
    )
    mine = gradient_mine(
        residual, keep, fixed_values, block_row, blocks, dp_count
    )
    summed = reduce_chunks(theirs, mine, half).astype(f16)
    fixed_grad = spread_chunks(summed, side, place, half, fixed_coef)
    return (margin.reshape(rows_here), updated_coef, fixed_grad)


def solution(mesh):
    placed = (
        P(("dp", "feat"), None),
        P(("dp", "feat")),
        P("dp", "feat"),
        P("dp", "feat"),
        P("feat", None),
        P(("dp", "feat"), None),
        P(("dp", "feat")),
        P(("dp", "feat")),
        P(("dp", "feat")),
    )
    return jax.shard_map(
        body,
        mesh=mesh,
        in_specs=placed,
        out_specs=(P(("dp", "feat")), P(("dp", "feat"), None), P("feat", None)),
        check_vma=False,
    )
```

```python
import jax
import jax.numpy as jnp
from jax import lax
from jax.experimental import pallas as pl
from jax.experimental.pallas import tpu as pltpu
from jax.sharding import PartitionSpec as P

CG_ITERS = 2
TILE = 128

ridge_member = 1.0
ridge_fixed = 1.0
bf16 = jnp.bfloat16
f32 = jnp.float32
f16 = jnp.float16


def split(value, parts):
    out = []
    for _ in range(parts):
        piece = value.astype(bf16)
        out.append(piece)
        value = value - piece.astype(f32)
    return out


def dot_nt(a, b):
    return lax.dot_general(a, b, (((1,), (1,)), ((), ())), preferred_element_type=f32)


def dot_nn(a, b):
    return jnp.dot(a, b, preferred_element_type=f32)


def rows_iota(shape):
    return lax.broadcasted_iota(jnp.int32, shape, 0)


def hot(index, count):
    return rows_iota((count, index.shape[1])) == index


def sigmoid(x):
    return 1.0 / (1.0 + jnp.exp(-x))


def compiler_params(mebibytes=50):
    return pltpu.CompilerParams(vmem_limit_bytes=mebibytes << 20)


def partial_kernel(
    values_ref, block_ref, coef_ref, label_ref, slot_ref, out_ref, keep_ref, held_ref, sem
):
    rows = out_ref.shape[1]
    blocks = coef_ref.shape[0]
    shards = values_ref.shape[0] // rows
    first = keep_ref.shape[0] // rows
    copies = [
        pltpu.make_async_copy(
            values_ref.at[pl.ds(i * rows, rows)],
            keep_ref.at[pl.ds(i * rows, rows)] if i < first else held_ref.at[i - first],
            sem.at[i],
        )
        for i in range(shards)
    ]
    for copy in copies:
        copy.start()
    high, low = split(coef_ref[...].T, 2)
    lanes = lax.broadcasted_iota(jnp.int32, (1, TILE), 1)
    out_ref[shards : shards + 1, :] = label_ref[...].astype(f32)
    out_ref[shards + 1 : shards + 2, :] = slot_ref[...].astype(f32)
    for i in range(shards):
        block = block_ref[:, i * rows : (i + 1) * rows]
        column = jnp.broadcast_to(block, (TILE, rows)).T
        copies[i].wait()
        values = keep_ref[i * rows : (i + 1) * rows, :] if i < first else held_ref[i - first]
        product = dot_nn(values, high) + dot_nn(values, low)
        total = jnp.zeros((rows, TILE), f32)
        for at in range(0, blocks, TILE):
            total = total + jnp.where(column == lanes + at, product[:, at : at + TILE], 0.0)
        out_ref[i : i + 1, :] = jnp.sum(total.T, axis=0, keepdims=True)


def partial_scores(fixed_values, block_row, fixed_coef, label_row, slot_row):
    rows, width = fixed_values.shape
    rows_here = slot_row.shape[1]
    blocks = fixed_coef.shape[0]
    shards = rows // rows_here
    first = shards // 2
    vmem = pl.BlockSpec(memory_space=pltpu.VMEM)
    return pl.pallas_call(
        partial_kernel,
        in_specs=[pl.BlockSpec(memory_space=pltpu.HBM)] + [vmem] * 4,
        out_specs=[vmem, vmem],
        out_shape=(
            jax.ShapeDtypeStruct((shards + 2, rows_here), f32),
            jax.ShapeDtypeStruct((first * rows_here, width), bf16),
        ),
        scratch_shapes=[
            pltpu.VMEM((shards - first, rows_here, width), bf16),
            pltpu.SemaphoreType.DMA((shards,)),
        ],
        cost_estimate=pl.CostEstimate(
            flops=4 * rows * blocks * width,
            bytes_accessed=2 * rows * width + 4 * blocks * width,
            transcendentals=0,
        ),
        compiler_params=compiler_params(50),
        name="partial_scores",
    )(fixed_values, block_row, fixed_coef, label_row, slot_row)


def add_blocks(
    flip, dp_count, shard_values, block_ref, residual_rows, out_ref
):
    kept = out_ref.shape[0]
    chunk = 2 * kept // dp_count
    rows = residual_rows[0].shape[1]
    parity = (lax.axis_index("dp") + flip) % 2
    place = lax.axis_index("dp") // 2
    for i, residual in enumerate(residual_rows):
        block = block_ref[:, i * rows : (i + 1) * rows]
        local = ((block // (2 * chunk)) ^ place) * chunk + block % chunk
        local = jnp.where((block // chunk) % 2 == parity, local, -1)
        mask = hot(local, kept)
        high, low = split(residual, 2)
        left_high = jnp.where(mask, high.astype(f32), 0.0).astype(bf16)
        left_low = jnp.where(mask, low.astype(f32), 0.0).astype(bf16)
        values = shard_values(i)
        total = dot_nn(left_high, values) + dot_nn(left_low, values)
        if i == 0:
            out_ref[...] = total
        else:
            out_ref[...] += total


def lookup_products(returned_ref, slot, shards, shard):
    sources, _, capacity = returned_ref.shape
    table = jnp.concatenate(split(returned_ref[...].reshape(sources, capacity), 3), axis=0)
    owner = slot // capacity
    place_hot = jnp.where(hot(slot - owner * capacity, capacity), 1.0, 0.0).astype(bf16)
    found = dot_nn(table, place_hot)
    found = found[:sources] + (found[sources : 2 * sources] + found[2 * sources :])
    owner_hot = hot(owner * shards + shard, sources)
    return jnp.sum(jnp.where(owner_hot, found, 0.0), axis=0, keepdims=True)


def lookup_lanes(returned_ref, slot, shards, shard):
    sources, _, capacity = returned_ref.shape
    rows = slot.shape[1]
    folds = rows // TILE
    slot = jnp.concatenate([slot[:, i * TILE : (i + 1) * TILE] for i in range(folds)], axis=0)
    block = slot // TILE
    lane = slot % TILE
    score = jnp.zeros(slot.shape, f32)
    per_owner = capacity // TILE
    for owner in range(sources // shards):
        for part in range(per_owner):
            piece = returned_ref[owner * shards + shard, :, part * TILE : (part + 1) * TILE]
            spread = jnp.broadcast_to(piece, slot.shape)
            found = jnp.take_along_axis(spread, lane, axis=1)
            score = jnp.where(block == owner * per_owner + part, found, score)
    return jnp.concatenate([score[i : i + 1] for i in range(folds)], axis=1)


def margin_kernel(
    dp_count, returned_ref, fixed_ref, label_ref, slot_ref, keep_ref, values_ref, block_ref,
    margin_ref, residual_ref, out_ref, all_ref, held_ref, sem,
):
    kept = keep_ref.shape[0]
    copy = pltpu.make_async_copy(values_ref.at[pl.ds(kept, held_ref.shape[0])], held_ref, sem)
    copy.start()
    capacity = returned_ref.shape[2]
    shards, rows = fixed_ref.shape
    lookup = lookup_lanes if capacity % TILE == 0 else lookup_products
    residual_rows = []
    for i in range(shards):
        slot = slot_ref[i : i + 1, :].astype(jnp.int32)
        score = lookup(returned_ref, slot, shards, i)
        margin = fixed_ref[i : i + 1, :] + score
        all_ref[i : i + 1, :] = margin
        residual = (label_ref[i : i + 1, :] - sigmoid(margin)) * (2.0 / dp_count)
        residual_ref[i : i + 1, :] = residual
        residual_rows.append(residual)
    margin_ref[...] = all_ref[pl.ds(lax.axis_index("feat"), 1), :]

    def shard_values(i):
        if i * rows == kept:
            copy.wait()
        if i * rows < kept:
            return keep_ref[i * rows : (i + 1) * rows, :]
        return held_ref[i * rows - kept : (i + 1) * rows - kept, :]

    add_blocks(1, dp_count, shard_values, block_ref, residual_rows, out_ref)


def margins_and_theirs(
    returned, fixed, label, slot, keep, fixed_values, block_row, blocks, dp_count
):
    shards, rows = fixed.shape
    group_rows, width = fixed_values.shape
    kept = keep.shape[0]

    def kernel(*refs):
        margin_kernel(dp_count, *refs)

    vmem = pl.BlockSpec(memory_space=pltpu.VMEM)
    return pl.pallas_call(
        kernel,
        in_specs=[vmem] * 5 + [pl.BlockSpec(memory_space=pltpu.HBM), vmem],
        out_specs=[vmem] * 3,
        out_shape=(
            jax.ShapeDtypeStruct((1, rows), f32),
            jax.ShapeDtypeStruct((shards, rows), f32),
            jax.ShapeDtypeStruct((blocks // 2, width), f32),
        ),
        scratch_shapes=[
            pltpu.VMEM((shards, rows), f32),
            pltpu.VMEM((group_rows - kept, width), bf16),
            pltpu.SemaphoreType.DMA,
        ],
        compiler_params=compiler_params(50),
        name="margins_and_theirs",
    )(returned, fixed, label, slot, keep, fixed_values, block_row)


def mine_kernel(
    dp_count, residual_ref, keep_ref, values_ref, block_ref, out_ref, held_ref, sem
):
    shards, rows = residual_ref.shape
    first = keep_ref.shape[0] // rows
    copies = [
        pltpu.make_async_copy(
            values_ref.at[pl.ds(i * rows, rows)], held_ref.at[i - first], sem.at[i - first]
        )
        for i in range(first, shards)
    ]
    for copy in copies:
        copy.start()

    def shard_values(i):
        if i < first:
            return keep_ref[i * rows : (i + 1) * rows, :]
        copies[i - first].wait()
        return held_ref[i - first]

    residual_rows = [residual_ref[i : i + 1, :] for i in range(shards)]
    add_blocks(0, dp_count, shard_values, block_ref, residual_rows, out_ref)


def gradient_mine(residual, keep, fixed_values, block_row, blocks, dp_count):
    rows, width = fixed_values.shape
    shards, rows_here = residual.shape
    copied = shards - keep.shape[0] // rows_here
    vmem = pl.BlockSpec(memory_space=pltpu.VMEM)
    hbm = pl.BlockSpec(memory_space=pltpu.HBM)

    def kernel(*refs):
        mine_kernel(dp_count, *refs)

    return pl.pallas_call(
        kernel,
        in_specs=[vmem, vmem, hbm, vmem],
        out_specs=vmem,
        out_shape=jax.ShapeDtypeStruct((blocks // 2, width), f32),
        scratch_shapes=[
            pltpu.VMEM((copied, rows_here, width), bf16),
            pltpu.SemaphoreType.DMA((copied,)),
        ],
        cost_estimate=pl.CostEstimate(
            flops=2 * rows * blocks * width,
            bytes_accessed=2 * rows * width + 2 * blocks * width,
            transcendentals=0,
        ),
        compiler_params=compiler_params(50),
        name="gradient_mine",
    )(residual, keep, fixed_values, block_row)


def pack_kernel(feats_in_ref, slot_in_ref, out_ref, feats_ref, slot_ref, held_ref, sem):
    loads = [
        pltpu.make_async_copy(slot_in_ref, slot_ref, sem.at[0]),
        pltpu.make_async_copy(feats_in_ref, feats_ref, sem.at[1]),
    ]
    for load in loads:
        load.start()
    for load in loads:
        load.wait()
    pieces, step, _ = held_ref.shape
    stores = []
    for i in range(pieces):
        mask = (rows_iota((step, slot_ref.shape[1])) + i * step) == slot_ref[...]
        one_hot = jnp.where(mask, 1.0, 0.0).astype(bf16)
        held_ref[i] = dot_nn(one_hot, feats_ref[...]).astype(bf16)
        stores.append(
            pltpu.make_async_copy(held_ref.at[i], out_ref.at[pl.ds(i * step, step)], sem.at[2 + i])
        )
        stores[-1].start()
    for store in stores:
        store.wait()


def pack_feats(member_feats, slot_row, slot_total):
    rows, width = member_feats.shape
    step = min(512, slot_total)
    pieces = slot_total // step
    hbm = pl.BlockSpec(memory_space=pltpu.HBM)
    return pl.pallas_call(
        pack_kernel,
        in_specs=[hbm, hbm],
        out_specs=hbm,
        out_shape=jax.ShapeDtypeStruct((slot_total, width), bf16),
        scratch_shapes=[
            pltpu.VMEM((rows, width), bf16),
            pltpu.VMEM((1, rows), jnp.int32),
            pltpu.VMEM((pieces, step, width), bf16),
            pltpu.SemaphoreType.DMA((2 + pieces,)),
        ],
        cost_estimate=pl.CostEstimate(
            flops=2 * rows * slot_total * width,
            bytes_accessed=2 * rows * width + 2 * slot_total * width,
            transcendentals=0,
        ),
        name="pack_feats",
    )(member_feats, slot_row)


def message_kernel(pieces, label_ref, slot_ref, fixed_ref, labels_ref, slots_ref, out_ref):
    shards = fixed_ref.shape[0]
    feat = lax.axis_index("feat")
    fixed = pieces[0][:shards, :]
    for piece in pieces[1:]:
        fixed = fixed + piece[:shards, :]
    fixed_ref[...] = fixed
    for k, piece in enumerate(pieces):
        labels_ref[pl.ds(feat ^ k, 1), :] = piece[shards : shards + 1, :]
        slots_ref[pl.ds(feat ^ k, 1), :] = piece[shards + 1 : shards + 2, :]
    destinations, _, capacity = out_ref.shape
    slot = slot_ref[...]
    owner = slot // capacity
    owner_hot = hot(owner, destinations)
    place_hot = jnp.where(hot(slot - owner * capacity, capacity), 1.0, 0.0).astype(bf16)
    score = fixed_ref[pl.ds(feat, 1), :].astype(bf16).astype(f32)
    label = label_ref[...].astype(f32)
    both = jnp.concatenate(
        [jnp.where(owner_hot, score, 0.0), jnp.where(owner_hot, label, 0.0)], axis=0
    )
    placed = dot_nt(both.astype(bf16), place_hot)
    out_ref[:, 0, :] = placed[:destinations]
    out_ref[:, 1, :] = placed[destinations:]


def build_message(pieces, label_row, slot_row, dp_count, capacity):
    rows = slot_row.shape[1]
    shards = len(pieces)

    def kernel(*refs):
        message_kernel(refs[:shards], *refs[shards:])

    return pl.pallas_call(
        kernel,
        out_shape=[jax.ShapeDtypeStruct((shards, rows), f32)] * 3
        + [jax.ShapeDtypeStruct((dp_count, 2, capacity), f32)],
        compiler_params=compiler_params(),
        name="build_message",
    )(*pieces, label_row, slot_row)


def slot_member_kernel(tiles_ref, source_ref, out_ref):
    slots, capacity = out_ref.shape
    source = source_ref[...]
    position = lax.broadcasted_iota(jnp.int32, source.shape, 1) // TILE
    member = jnp.zeros(source.shape, jnp.int32)
    end = jnp.int32(0)
    for m in range(tiles_ref.shape[0]):
        end = end + tiles_ref[m]
        member = member + (position >= end).astype(jnp.int32)
    sender = source // capacity
    sender_hot = jnp.where(hot(sender, slots), member.astype(f32) + 1.0, 0.0).astype(bf16)
    place_hot = jnp.where(hot(source - sender * capacity, capacity), 1.0, 0.0).astype(bf16)
    out_ref[...] = dot_nt(sender_hot, place_hot) - 1.0


def slot_members(member_tiles, source_row, dp_count, capacity):
    return pl.pallas_call(
        slot_member_kernel,
        in_specs=[
            pl.BlockSpec(memory_space=pltpu.SMEM),
            pl.BlockSpec(memory_space=pltpu.VMEM),
        ],
        out_specs=pl.BlockSpec(memory_space=pltpu.VMEM),
        out_shape=jax.ShapeDtypeStruct((dp_count, capacity), f32),
        compiler_params=compiler_params(),
        name="slot_members",
    )(member_tiles, source_row)


def lane_row(pieces):
    lanes = pieces.shape[-1]
    pieces = pieces.reshape(-1, lanes)
    return jnp.concatenate([pieces[i : i + 1] for i in range(pieces.shape[0])], axis=1)


def solve_kernel(feats_ref, message_ref, member_ref, coef_ref, updated_ref, scores_ref):
    feats = feats_ref[...]
    coef = coef_ref[...]
    count = coef.shape[0]
    slots = feats.shape[0]
    lanes = message_ref.shape[2]
    message = message_ref[...]
    sent_score = lane_row(message[:, 0, :])
    label = lane_row(message[:, 1, :])
    own = rows_iota((count, slots)).astype(f32) == lane_row(member_ref[...])

    def pick(vectors):
        high, low = split(vectors, 2)
        both = dot_nt(jnp.concatenate([high, low], axis=0), feats)
        each = both[:count] + both[count:]
        return jnp.sum(jnp.where(own, each, 0.0), axis=0, keepdims=True)

    def spread(row_weights):
        high, low = split(jnp.where(own, row_weights, 0.0), 2)
        return jnp.concatenate([high, low], axis=0)

    def gather(row_weights):
        both = dot_nn(spread(row_weights), feats)
        return both[:count] + both[count:]

    base = pick(coef)
    logits = sent_score + base
    probability = sigmoid(logits)
    weight = probability * (1.0 - probability)
    gradient = gather(label - probability) - ridge_member * coef
    wide = feats.astype(f32)
    square_high, square_low = split(wide * wide, 2)
    weights = spread(weight)
    both = dot_nn(weights, square_high) + dot_nn(weights, square_low)
    diagonal = both[:count] + both[count:] + ridge_member
    step_sum = jnp.zeros_like(coef)
    new_scores = base
    remain = gradient
    scaled = remain / diagonal
    search = scaled
    inner_product = jnp.sum(remain * scaled, axis=1, keepdims=True)
    for iteration in range(CG_ITERS):
        projected = pick(search)
        if iteration + 1 < CG_ITERS:
            image = gather(weight * projected) + ridge_member * search
            curvature = jnp.sum(search * image, axis=1, keepdims=True)
        else:
            row_part = jnp.where(own, weight * projected * projected, 0.0)
            curvature = jnp.sum(row_part, axis=1, keepdims=True) + ridge_member * jnp.sum(
                search * search, axis=1, keepdims=True
            )
        alpha_step = inner_product / curvature
        step_sum = step_sum + alpha_step * search
        row_alpha = jnp.sum(jnp.where(own, alpha_step, 0.0), axis=0, keepdims=True)
        new_scores = new_scores + row_alpha * projected
        if iteration + 1 < CG_ITERS:
            remain = remain - alpha_step * image
            scaled = remain / diagonal
            inner_next = jnp.sum(remain * scaled, axis=1, keepdims=True)
            search = scaled + (inner_next / inner_product) * search
            inner_product = inner_next
    updated_ref[...] = coef + step_sum
    copies = scores_ref.shape[0] * lanes // slots
    for i in range(slots // lanes):
        for copy in range(copies):
            scores_ref[i * copies + copy] = new_scores[:, i * lanes : (i + 1) * lanes]


def solve_members(feats, message, member_slots, member_coef, copies):
    senders, _, capacity = message.shape
    return pl.pallas_call(
        solve_kernel,
        out_shape=(
            jax.ShapeDtypeStruct(member_coef.shape, f32),
            jax.ShapeDtypeStruct((senders * copies, 1, capacity), f32),
        ),
        compiler_params=compiler_params(),
        name="solve_members",
    )(feats, message, member_slots, member_coef)


def swap(value, axis, offset):
    return lax.ppermute(
        value, axis, [(i, i ^ offset) for i in range(lax.axis_size(axis))]
    )


def pick_index(value, index):
    return lax.dynamic_index_in_dim(value, index, 0, keepdims=False)


def exchange(message, side, place, half):
    if half > 4:
        return lax.all_to_all(message, "dp", 0, 0, tiled=True)
    pairs = message.reshape((half, 2) + message.shape[1:])
    own = lax.dynamic_index_in_dim(pairs, side, 1, keepdims=False)
    other = swap(lax.dynamic_index_in_dim(pairs, 1 - side, 1, keepdims=False), "dp", 1)
    both = jnp.where(
        side == 0, jnp.stack([own, other], axis=1), jnp.stack([other, own], axis=1)
    )
    out = jnp.zeros_like(both)
    for k in range(half):
        entry = pick_index(both, place ^ k)
        got = entry if k == 0 else swap(entry, "dp", 2 * k)
        out = lax.dynamic_update_index_in_dim(out, got, place ^ k, 0)
    return out.reshape(message.shape)


def reduce_chunks(theirs, mine, half):
    chunk = mine.shape[0] // half
    sends = theirs.astype(f16)
    if half > 4:
        kept = mine + swap(sends, "dp", 1).astype(f32)
        low = half // 2
        while low:
            got = swap(kept[low * chunk :].astype(f16), "dp", 2 * low)
            kept = kept[: low * chunk] + got.astype(f32)
            low //= 2
        return kept
    order = [k for k in (1, 3, 2, 0) if k < half]
    got = {}
    for k in order:
        got[k] = swap(sends[k * chunk : (k + 1) * chunk], "dp", 1)
    landed = []
    before = None
    for k in order:
        other = got[k]
        if before is not None:
            other = lax.optimization_barrier((other, before))[0]
        kept = mine[k * chunk : (k + 1) * chunk] + other.astype(f32)
        if k == 0:
            total = kept
        else:
            before = kept.astype(f16)
            landed.append(swap(before, "dp", 2 * k))
    for piece in landed:
        total = total + piece.astype(f32)
    return total


def spread_chunks(own, side, place, half, coef):
    rows = own.shape[0]
    out = jnp.zeros(coef.shape, f32)

    def put(out, got, k, parity):
        at = ((place ^ k) * 2 + parity) * rows
        own_coef = lax.dynamic_slice_in_dim(coef, at, rows, 0)
        grad = ridge_fixed * own_coef - 0.5 * got.astype(f32)
        return lax.dynamic_update_slice_in_dim(out, grad, at, 0)

    if half > 4:
        whole = own
        low = 1
        while low < half:
            whole = jnp.concatenate([whole, swap(whole, "dp", 2 * low)])
            low *= 2
        other = swap(whole, "dp", 1)
        for k in range(half):
            at = slice(k * rows, (k + 1) * rows)
            out = put(out, whole[at], k, side)
            out = put(out, other[at], k, 1 - side)
        return out
    same = {0: own}
    order = [k for k in (1, 3, 2) if k < half]
    for k in order:
        same[k] = swap(own, "dp", 2 * k)
    for k in (0, *order):
        other = swap(same[k], "dp", 1)
        pair = jnp.where(
            side == 0,
            jnp.concatenate([same[k], other]),
            jnp.concatenate([other, same[k]]),
        )
        at = (place ^ k) * 2 * rows
        own_coef = lax.dynamic_slice_in_dim(coef, at, 2 * rows, 0)
        grad = ridge_fixed * own_coef - 0.5 * pair.astype(f32)
        out = lax.dynamic_update_slice_in_dim(out, grad, at, 0)
    return out


def body(
    member_feats,
    labels,
    fixed_values,
    fixed_blocks,
    fixed_coef,
    member_coef,
    row_slot,
    tile_source,
    member_tiles,
):
    dp_count = lax.axis_size("dp")
    feat_count = lax.axis_size("feat")
    rows_here = member_feats.shape[0]
    blocks = fixed_coef.shape[0]
    capacity = 2 * rows_here // dp_count
    slot_total = dp_count * capacity
    group_rows = fixed_values.shape[0]
    side = lax.axis_index("dp") % 2
    place = lax.axis_index("dp") // 2
    half = dp_count // 2

    slot_row = row_slot.reshape(1, rows_here)
    label_row = labels.reshape(1, rows_here)
    block_row = fixed_blocks.reshape(1, group_rows)

    send_feats = pack_feats(member_feats, slot_row, slot_total)
    got_feats = lax.all_to_all(
        send_feats.reshape(dp_count, capacity, -1), "dp", 0, 0, tiled=True
    ).reshape(slot_total, -1)
    member_slots = slot_members(
        member_tiles, tile_source.reshape(1, -1), dp_count, capacity
    )

    own, keep = partial_scores(fixed_values, block_row, fixed_coef, label_row, slot_row)
    pieces = [own] + [swap(own, "feat", k) for k in range(1, feat_count)]
    fixed, label, slot, message = build_message(
        pieces, label_row, slot_row, dp_count, capacity
    )
    got = exchange(message, side, place, half)

    if capacity % 128:
        got = jnp.moveaxis(got, 1, 0).reshape(1, 2, slot_total)
        member_slots = member_slots.reshape(1, slot_total)
        updated_coef, new_scores = solve_members(got_feats, got, member_slots, member_coef, 1)
        new_scores = jnp.broadcast_to(
            new_scores.reshape(dp_count, 1, 1, capacity), (dp_count, feat_count, 1, capacity)
        ).reshape(dp_count * feat_count, 1, capacity)
    else:
        updated_coef, new_scores = solve_members(
            got_feats, got, member_slots, member_coef, feat_count
        )
    returned = lax.all_to_all(new_scores, ("dp", "feat"), 0, 0, tiled=True)
    margin, residual, theirs = margins_and_theirs(
        returned, fixed, label, slot, keep, fixed_values, block_row, blocks, dp_count
    )
    mine = gradient_mine(
        residual, keep, fixed_values, block_row, blocks, dp_count
    )
    summed = reduce_chunks(theirs, mine, half).astype(f16)
    fixed_grad = spread_chunks(summed, side, place, half, fixed_coef)
    return (margin.reshape(rows_here), updated_coef, fixed_grad)


def solution(mesh):
    placed = (
        P(("dp", "feat"), None),
        P(("dp", "feat")),
        P("dp", "feat"),
        P("dp", "feat"),
        P("feat", None),
        P(("dp", "feat"), None),
        P(("dp", "feat")),
        P(("dp", "feat")),
        P(("dp", "feat")),
    )
    return jax.shard_map(
        body,
        mesh=mesh,
        in_specs=placed,
        out_specs=(P(("dp", "feat")), P(("dp", "feat"), None), P("feat", None)),
        check_vma=False,
    )
```
